32 devices in a mesh: gx: 8 (over z, core), gy: 4 (over y, x).
Axes of the slice: x: 2, y: 2, z: 4, core: 2. Of those that a mesh axis runs over, the one named last changes fastest.
Arguments:
- initial_temp: float32 [16, 64, 512], P(None, 'gx', 'gy'), may hold values from 0.85 to 1.2
- material: int32 [16, 64, 512], P(None, 'gx', 'gy'), may hold values from 0 to 15
- plate: int32 [16, 64, 512], P(None, 'gx', 'gy'), may hold values 0 or 1
- cooling: float32 [16, 64, 512], P(None, 'gx', 'gy'), may hold values from 0.02 to 0.1
- principal: float32 [16, 3], replicated, may hold values from 0.1 to 1
- angles: float32 [16, 3], replicated, may hold values from -3.140625 to 3.140625
- aging_scale: float32 [16], replicated, may hold values from 0.5 to 2
Outputs:
- temp_sensitivity: float32 [16, 64, 512], P(None, 'gx', 'gy')
- cooling_sensitivity: float32 [16, 64, 512], P(None, 'gx', 'gy')
The draws below stay inside these ranges and needn't reach their ends.
All inputs are finite; a program needn't handle non-finite values. No bound on the sum of `plate` on one device may be relied on, other than what follows from the above.
Results may differ from the reference program's by a relative error of at most 0.0003.
Values sent between devices are 32-bit elements; how exact they have to be, the bound alone decides.
No kernel may reach another device: no remote copies, remote signals or barrier semaphores. Data moves between devices by JAX's collectives and lax.ppermute only.
A program may use at most 64 MiB of HBM per device.

```python
import math
import jax
import jax.numpy as jnp
from jax import lax

NZ = 16
MATS = 16
STEPS = 3
NX = 64
NY = 512


def draw_initial_temp(key, part):
    ramp = (lax.broadcasted_iota(jnp.float32, (NZ, NX, NY), 1) + 0.5) / NX
    noise = 0.03 * jnp.clip(jax.random.normal(key, (NZ, NX, NY), jnp.float32), -1.6, 1.6)
    return 0.9 + 0.24 * ramp + noise


def plant(entries, stream_key, least, top_value):
    longest = entries.shape.index(max(entries.shape))
    spots = []
    for shift in (0, 1):
        where = [jax.random.randint(jax.random.fold_in(stream_key, axis), (), 0, length) for axis, length in enumerate(entries.shape)]
        where[longest] = (where[longest] + shift) % entries.shape[longest]
        spots.append(tuple(where))
    return entries.at[spots[0]].set(least).at[spots[1]].set(top_value)


def shard_levels(key, shape, shards, least, top_value):
    gain = 1.0
    for position, shards_of in shards:
        draws = jax.random.uniform(jax.random.fold_in(jax.random.fold_in(key, 6), position), (shards_of,), jnp.float32, least / len(shards), top_value / len(shards))
        gain = gain * jnp.repeat(jnp.exp(draws), shape[position] // shards_of).reshape((-1,) + (1,) * (len(shape) - 1 - position))
    return gain


def setup_inputs(seed: int = 0) -> dict:
    arg_keys = jax.random.split(jax.random.key(seed), 8)
    return {
        "initial_temp": draw_initial_temp(jax.random.fold_in(arg_keys[7], 71), 0),
        "material": plant(jax.random.randint(arg_keys[1], (NZ, NX, NY), 0, MATS), jax.random.fold_in(arg_keys[1], 1), 0, MATS - 1).astype(jnp.int32),
        "plate": plant((jax.random.randint(arg_keys[2], (NZ, NX, NY), 0, 4) < 1).astype(jnp.int32), jax.random.fold_in(arg_keys[2], 1), 0, 1),
        "cooling": jnp.clip(0.02 + 0.08 * jax.random.uniform(arg_keys[3], (NZ, NX, NY), jnp.float32) ** shard_levels(arg_keys[3], (NZ, NX, NY), ((1, 8), (2, 4)), -0.2, 0.2), 0.02, 0.1),
        "principal": jnp.clip(jnp.exp(jax.random.uniform(arg_keys[4], (MATS, 3), jnp.float32, math.log(0.1), math.log(1.0))), 0.1, 1.0),
        "angles": jnp.clip(jax.random.uniform(arg_keys[5], (MATS, 3), jnp.float32, -3.140625, 3.140625), -3.140625, 3.140625),
        "aging_scale": jnp.clip(jnp.exp(jax.random.uniform(arg_keys[6], (MATS,), jnp.float32, math.log(0.5), math.log(2.0))), 0.5, 2.0),
    }


STEP_SCALE = 0.06
COOL_TEMP = 0.85
AGE_BETA = 8.0
HALF_OFFSETS = [(first, second, third) for first in (-1, 0, 1) for second in (-1, 0, 1) for third in (-1, 0, 1) if (first, second, third) > (0, 0, 0)]


def weight_table(principal, angles, aging_scale):
    cos_first = jnp.cos(angles[:, 0])
    sin_first = jnp.sin(angles[:, 0])
    cos_second = jnp.cos(angles[:, 1])
    sin_second = jnp.sin(angles[:, 1])
    cos_third = jnp.cos(angles[:, 2])
    sin_third = jnp.sin(angles[:, 2])
    columns = [
        (cos_first * cos_third - sin_first * cos_second * sin_third, sin_first * cos_third + cos_first * cos_second * sin_third, sin_second * sin_third),
        (-cos_first * sin_third - sin_first * cos_second * cos_third, -sin_first * sin_third + cos_first * cos_second * cos_third, sin_second * cos_third),
        (sin_first * sin_second, -cos_first * sin_second, cos_second),
    ]
    rows = []
    for offset in HALF_OFFSETS:
        length_sq = float(offset[0] ** 2 + offset[1] ** 2 + offset[2] ** 2)
        kappa = jnp.zeros_like(aging_scale)
        for index in range(3):
            along = columns[index][0] * offset[0] + columns[index][1] * offset[1] + columns[index][2] * offset[2]
            kappa = kappa + principal[:, index] * along * along
        rows.append(STEP_SCALE * kappa / (length_sq * length_sq))
    rows.append(aging_scale)
    return jnp.stack(rows, 0)


def beside_all(padded, offset, sign):
    size_z = padded.shape[0] - 2
    size_x = padded.shape[1] - 2
    size_y = padded.shape[2] - 2
    start_z = 1 + sign * offset[0]
    start_x = 1 + sign * offset[1]
    start_y = 1 + sign * offset[2]
    return padded[start_z:start_z + size_z, start_x:start_x + size_x, start_y:start_y + size_y]


def reference(initial_temp, material, plate, cooling, principal, angles, aging_scale):
    table = weight_table(principal, angles, aging_scale)
    links = len(HALF_OFFSETS)
    coeff = cooling * plate.astype(jnp.float32)
    valid = jnp.pad(jnp.ones_like(initial_temp), 1)
    material_pad = jnp.pad(material, 1)
    diag = coeff
    for index, offset in enumerate(HALF_OFFSETS):
        diag = diag + jnp.take(table[index], material) * (beside_all(valid, offset, 1) + beside_all(valid, offset, -1))
    aging = jnp.take(table[links], material)
    temps = [initial_temp]
    current = initial_temp
    for step in range(STEPS):
        padded = jnp.pad(current, 1)
        near = jnp.zeros_like(current)
        for index, offset in enumerate(HALF_OFFSETS):
            near = near + jnp.take(table[index], material) * (beside_all(padded, offset, 1) + beside_all(padded, offset, -1))
        current = (1.0 - diag) * current + near + coeff * COOL_TEMP
        temps.append(current)
    total = jnp.zeros((), jnp.float32)
    drives = []
    for state in temps[1:]:
        rate = jnp.exp(AGE_BETA * (1.0 - 1.0 / state))
        total = total + jnp.sum(aging * rate)
        drives.append(aging * AGE_BETA * rate / (state * state))

    def transpose(adjoint):
        padded = jnp.pad(adjoint, 1)
        result = (1.0 - diag) * adjoint
        for index, offset in enumerate(HALF_OFFSETS):
            product = jnp.take(table[index], material_pad) * padded
            result = result + beside_all(product, offset, -1) + beside_all(product, offset, 1)
        return result

    adjoint = drives[-1]
    sens = jnp.zeros_like(initial_temp)
    for step in range(STEPS - 1, -1, -1):
        sens = sens - adjoint * (temps[step] - COOL_TEMP)
        adjoint = transpose(adjoint)
        if step > 0:
            adjoint = adjoint + drives[step - 1]
    scale = float(NZ * NX * NY) / total
    return adjoint * scale, sens * plate.astype(jnp.float32) * scale
```

```python
import functools

import jax
import jax.numpy as jnp
from jax import lax
from jax.experimental import pallas as pl
from jax.experimental.pallas import tpu as pltpu
from jax.sharding import PartitionSpec as P

STEPS = 3
STEP_SCALE = 0.06
COOL_TEMP = 0.85
AGE_BETA = 8.0
HALF_OFFSETS = [
    (first, second, third)
    for first in (-1, 0, 1)
    for second in (-1, 0, 1)
    for third in (-1, 0, 1)
    if (first, second, third) > (0, 0, 0)
]
LINKS = len(HALF_OFFSETS)
HALO = 2 * STEPS
LANES = 128
SLOT = 16
T0, ID, COEFF = 0, 1, 2
VMEM = pl.BlockSpec(memory_space=pltpu.VMEM)


def table_rows(raw):
    angles = raw[3:6]
    cosine, sine = jnp.cos(angles), jnp.sin(angles)
    c1, c2, c3 = cosine[0:1], cosine[1:2], cosine[2:3]
    s1, s2, s3 = sine[0:1], sine[1:2], sine[2:3]
    columns = [
        (c1 * c3 - s1 * c2 * s3, s1 * c3 + c1 * c2 * s3, s2 * s3),
        (-c1 * s3 - s1 * c2 * c3, -s1 * s3 + c1 * c2 * c3, s2 * c3),
        (s1 * s2, -c1 * s2, c2),
    ]
    rows = []
    for offset in HALF_OFFSETS:
        length_sq = float(offset[0] ** 2 + offset[1] ** 2 + offset[2] ** 2)
        kappa = jnp.zeros_like(c1)
        for index in range(3):
            along = (
                columns[index][0] * offset[0]
                + columns[index][1] * offset[1]
                + columns[index][2] * offset[2]
            )
            kappa = kappa + raw[index : index + 1] * along * along
        rows.append(STEP_SCALE * kappa / (length_sq * length_sq))
    rows.append(raw[6:7])
    return rows


def lane_of(shape):
    return lax.broadcasted_iota(jnp.int32, shape, len(shape) - 1)


def pack_kernel(temp, material, plate, cooling, raw, own, send_a, send_b, pack, table):
    depth, rows, _ = temp.shape
    lane = lane_of((depth, LANES))
    packs = [jnp.zeros((depth, LANES), jnp.float32) for _ in range(3)]
    for x in range(rows):
        fields = (
            temp[:, x, :],
            (material[:, x, :] + 1).astype(jnp.float32),
            cooling[:, x, :] * plate[:, x, :].astype(jnp.float32),
        )
        mine = (lane >= SLOT * x) & (lane < SLOT * (x + 1))
        for f in range(3):
            own[f, x] = fields[f]
            moved = pltpu.roll(fields[f], (SLOT * x + HALO) % LANES, 1)
            packs[f] = jnp.where(mine, moved, packs[f])
    even = lax.rem(lax.axis_index("gx"), 2) == 0
    first_a = jnp.where(even, rows - HALO, 0)
    first_b = jnp.where(even, 0, rows - HALO)
    for f in range(3):
        pack[f] = packs[f]
        for r in range(HALO):
            send_a[f, r] = own[f, first_a + r]
            send_b[f, r] = own[f, first_b + r]
    for k, row in enumerate(table_rows(raw)):
        table[k] = jnp.broadcast_to(row, (8, LANES))


class Field:
    def __init__(self):
        self.where = {}

    def add(self, ref, rows, lead=(), first=None):
        for r in rows:
            self.where[r] = (ref, (*lead, r if first is None else r - first))

    def get(self, r, t, start=None, size=16):
        ref, index = self.where[r]
        if start is None:
            return ref[(*index, t)]
        return ref[(*index, t, pl.ds(start, size))]

    def put(self, r, t, value, start=None):
        ref, index = self.where[r]
        if start is None:
            ref[(*index, t)] = value
        else:
            ref[(*index, t, pl.ds(start, value.shape[0]))] = value


PAD = 8
DEPTH_PAD = 8 + 16 + 8


def clear_pads(field, rows, depth, tiles=(0, 1)):
    zero = jnp.zeros((8, LANES), jnp.float32)
    for r in rows:
        for t in tiles:
            field.put(r, t, zero, 0)
            field.put(r, t, zero, PAD + depth)


def lane_shift(pair, by):
    lane = lane_of(pair[0].shape)
    moved = [pltpu.roll(value, (-by) % LANES, 1) for value in pair]
    edge = lane == (LANES - 1 if by > 0 else 0)
    return [jnp.where(edge, moved[1 - t], moved[t]) for t in (0, 1)]


def put_shifted(fields, r, pair):
    for by in (-1, 0, 1):
        moved = pair if by == 0 else lane_shift(pair, by)
        for t in (0, 1):
            fields[by].put(r, t, moved[t], PAD)


def near_sum(weights, fields, r, t, depth, cache):
    total = None

    def read(oz, ox, oy):
        key = (oz, r + ox, oy, t)
        if key not in cache:
            cache[key] = fields[oy].get(r + ox, t, PAD + oz, depth)
        return cache[key]

    for k, (oz, ox, oy) in enumerate(HALF_OFFSETS):
        term = weights[k].get(r, t, PAD, depth) * (read(oz, ox, oy) + read(-oz, -ox, -oy))
        total = term if total is None else total + term
    return total


def expand(table, weights, ids, rows, depth):
    for r in rows:
        for t in (0, 1):
            index = ids.get(r, t).astype(jnp.int32)
            for half in range(depth // 8):
                part = index[8 * half : 8 * half + 8]
                for k in range(LINKS + 1):
                    got = jnp.take_along_axis(
                        table[k], part, axis=1, mode="promise_in_bounds"
                    )
                    weights[k].put(r, t, got, PAD + 8 * half)


def rate_of(state):
    good = state > 0.5
    inverse = 1.0 / jnp.where(good, state, 1.0)
    return jnp.where(good, jnp.exp(AGE_BETA * (1.0 - inverse)), 0.0), inverse


class Plan:
    def __init__(self, rows):
        self.rows = rows
        self.all = range(rows + 2 * HALO)

    def cone(self, radius):
        return range(HALO - radius, HALO + self.rows + radius)

    def ring(self, radius, inner):
        middle = self.cone(inner)
        return [r for r in self.cone(radius) if r not in middle]


def front_kernel(
    own, got_a, got_b, mid, mid_a, mid_b, table,
    ext, weights_ref, diag_ref, shifted_ref, third_ref, part,
    valid_ref,
):
    _, rows, depth, _ = own.shape
    plan = Plan(rows)
    even = lax.rem(lax.axis_index("gx"), 2) == 0
    base_a = jnp.where(even, HALO + rows, 0)
    base_b = jnp.where(even, 0, HALO + rows)
    lane = lane_of((depth, LANES))
    halo_lane = (lane < HALO) | (lane >= LANES - HALO)
    for f in range(3):
        for r in range(HALO):
            ext[f, base_a + r, 0] = got_a[f, r]
            ext[f, base_b + r, 0] = got_b[f, r]
        for x in range(rows):
            ext[f, HALO + x, 0] = own[f, x]
        low = jnp.where(even, mid_b[f], mid_a[f])
        high = jnp.where(even, mid_a[f], mid_b[f])
        for r in plan.all:
            x = r - HALO
            source, x = (
                (low, x + rows) if x < 0 else (high, x - rows) if x >= rows else (mid[f], x)
            )
            moved = pltpu.roll(source, (-(SLOT * x + HALO)) % LANES, 1)
            ext[f, r, 1] = jnp.where(halo_lane, moved, 0.0)

    temp, ids, coeff = Field(), Field(), Field()
    for field, f in ((temp, T0), (ids, ID), (coeff, COEFF)):
        field.add(ext, plan.all, (f,))
    weights = [Field() for _ in range(LINKS + 1)]
    for k in range(LINKS + 1):
        weights[k].add(weights_ref, plan.cone(2), (k,), HALO - 2)
        clear_pads(weights[k], plan.cone(2), depth)
    diag = Field()
    diag.add(diag_ref, plan.cone(2), (), HALO - 2)
    valid = {}
    shifted = []
    for oy in (-1, 0, 1):
        valid[oy] = Field()
        valid[oy].add(valid_ref, plan.cone(3), (oy + 1,), HALO - 3)
        clear_pads(valid[oy], plan.cone(3), depth)
    for n in range(3):
        shifted.append({})
        for oy in (-1, 0, 1):
            shifted[n][oy] = Field()
            shifted[n][oy].add(shifted_ref, plan.cone(3 - n), (n, oy + 1), HALO - 3)
            clear_pads(shifted[n][oy], plan.cone(3 - n), depth)

    expand(table, weights, ids, plan.cone(2), depth)
    for r in plan.cone(3):
        put_shifted(valid, r, [jnp.where(ids.get(r, t) > 0.5, 1.0, 0.0) for t in (0, 1)])
        put_shifted(shifted[0], r, [temp.get(r, t) for t in (0, 1)])
    cache = {}
    for r in plan.cone(2):
        for t in (0, 1):
            diag.put(r, t, coeff.get(r, t) + near_sum(weights, valid, r, t, depth, cache))
    loss = jnp.zeros((depth, LANES), jnp.float32)
    for n in range(STEPS):
        cache = {}
        for r in plan.cone(2 - n):
            pair = []
            for t in (0, 1) if n < 2 else (0,):
                center = shifted[n][0].get(r, t, PAD, depth)
                near = near_sum(weights, shifted[n], r, t, depth, cache)
                pair.append(
                    (1.0 - diag.get(r, t)) * center + near + coeff.get(r, t) * COOL_TEMP
                )
            if n < 2:
                put_shifted(shifted[n + 1], r, pair)
            else:
                third_ref[r - HALO] = pair[0]
            if HALO <= r < HALO + rows:
                rate, _ = rate_of(pair[0])
                loss = loss + weights[LINKS].get(r, 0, PAD, depth) * rate
    part[...] = jnp.broadcast_to(jnp.sum(loss, axis=0, keepdims=True), part.shape)


def back_kernel(
    ext, weights_in, diag_in, shifted_in, third_in, table,
    adjoint_out, sens_out,
    weights_ref, diag_ref, valid_ref, shifted_ref, state_ref, adjoint_ref,
):
    rows = third_in.shape[0]
    depth = third_in.shape[1]
    plan = Plan(rows)
    temp, ids, coeff = Field(), Field(), Field()
    for field, f in ((temp, T0), (ids, ID), (coeff, COEFF)):
        field.add(ext, plan.all, (f,))
    outer = plan.ring(5, 2)
    slot = {r: (r - 1 if r < HALO else r - rows - 5) for r in outer}

    def ring_field(ref, lead, rows_):
        field = Field()
        for r in rows_:
            field.where[r] = (ref, (*lead, slot[r]))
        return field

    weights = []
    for k in range(LINKS + 1):
        field = ring_field(weights_ref, (k,), outer)
        clear_pads(field, [r for r in outer if r in plan.cone(3)], depth)
        field.add(weights_in, plan.cone(2), (k,), HALO - 2)
        weights.append(field)
    diag = ring_field(diag_ref, (), outer)
    diag.add(diag_in, plan.cone(2), (), HALO - 2)
    valid, shifted = {}, [{}, {}, {}]
    valid_rows = [r for r in plan.all if r not in plan.cone(1)]
    for oy in (-1, 0, 1):
        valid[oy] = Field()
        for i, r in enumerate(valid_rows):
            valid[oy].where[r] = (valid_ref, (oy + 1, i))
        clear_pads(valid[oy], valid_rows, depth)
        for n in range(3):
            shifted[n][oy] = Field()
            inner = plan.cone(3 - n)
            fresh = plan.ring(6 - n, 3 - n)
            for i, r in enumerate(fresh):
                shifted[n][oy].where[r] = (shifted_ref, (n, oy + 1, i))
            clear_pads(shifted[n][oy], fresh, depth)
            shifted[n][oy].add(shifted_in, inner, (n, oy + 1), HALO - 3)

    expand(table, weights, ids, outer, depth)
    for r in valid_rows:
        put_shifted(valid, r, [jnp.where(ids.get(r, t) > 0.5, 1.0, 0.0) for t in (0, 1)])
    for r in plan.ring(6, 3):
        put_shifted(shifted[0], r, [temp.get(r, t) for t in (0, 1)])
    cache = {}
    for r in outer:
        for t in (0, 1):
            diag.put(r, t, coeff.get(r, t) + near_sum(weights, valid, r, t, depth, cache))
    third = Field()
    third.add(state_ref, plan.cone(3), (), HALO - 3)
    for n in range(STEPS):
        cache = {}
        todo = [(r, t) for r in plan.ring(5 - n, 2 - n) for t in (0, 1)]
        if n == 2:
            todo = todo + [(r, 1) for r in plan.cone(0)]
        pair = {}
        for r, t in todo:
            center = shifted[n][0].get(r, t, PAD, depth)
            near = near_sum(weights, shifted[n], r, t, depth, cache)
            value = (1.0 - diag.get(r, t)) * center + near + coeff.get(r, t) * COOL_TEMP
            if n == 2:
                third.put(r, t, value)
                continue
            pair[t] = value
            if t == 1:
                put_shifted(shifted[n + 1], r, [pair[0], pair[1]])
    for r in plan.cone(0):
        third.put(r, 0, third_in[r - HALO])

    def state_of(n, r, t):
        return third.get(r, t) if n == 3 else shifted[n][0].get(r, t, PAD, depth)

    def drive(n, r, t):
        rate, inverse = rate_of(state_of(n, r, t))
        return weights[LINKS].get(r, t, PAD, depth) * AGE_BETA * rate * (inverse * inverse)

    vectors = []
    for n in range(3):
        field = Field()
        field.add(adjoint_ref, plan.cone(3 - n), (n,), HALO - 3)
        clear_pads(field, plan.cone(3 - n), depth)
        vectors.append(field)
    for r in plan.cone(3):
        for t in (0, 1):
            vectors[0].put(r, t, drive(3, r, t), PAD)
    sens = {r: jnp.zeros((depth, LANES), jnp.float32) for r in plan.cone(0)}
    for n in range(3):
        vector = vectors[n]
        sums = {}
        for source in plan.cone(3 - n):
            for t in (0, 1):
                reads = {oz: vector.get(source, t, PAD - oz, depth) for oz in (-1, 0, 1)}
                for k, offset in enumerate(HALF_OFFSETS):
                    product = {}
                    for sign in (1, -1):
                        oz, ox, oy = (sign * o for o in offset)
                        target = source + ox
                        if oz not in product:
                            product[oz] = reads[oz] * weights[k].get(source, t, PAD - oz, depth)
                        if target in plan.cone(2 - n):
                            key = (target, oy, t)
                            sums[key] = sums[key] + product[oz] if key in sums else product[oz]
            target = source - 1
            if target not in plan.cone(2 - n):
                continue
            plus = lane_shift([sums.pop((target, 1, t)) for t in (0, 1)], -1)
            minus = lane_shift([sums.pop((target, -1, t)) for t in (0, 1)], 1)
            for t in (0, 1) if n < 2 else (0,):
                result = (
                    (1.0 - diag.get(target, t)) * vector.get(target, t, PAD, depth)
                    + sums.pop((target, 0, t))
                    + (plus[t] + minus[t])
                )
                if n < 2:
                    vectors[n + 1].put(target, t, result + drive(2 - n, target, t), PAD)
                else:
                    adjoint_out[:, target - HALO, :] = result
    for r in plan.cone(0):
        total = None
        for n in range(3):
            term = vectors[2 - n].get(r, 0, PAD, depth) * (state_of(n, r, 0) - COOL_TEMP)
            total = term if total is None else total + term
        sens_out[:, r - HALO, :] = -total


def pairing(count, first):
    out = {}
    for i in range(first, count - 1, 2):
        out[i], out[i + 1] = i + 1, i
    return out


def swap(value, sizes, axis, first):
    count_x, count_y = sizes
    partner = pairing(sizes[axis], first)
    pairs = []
    for i in range(count_x):
        for j in range(count_y):
            other = partner.get((i, j)[axis])
            if other is not None:
                target = (other, j) if axis == 0 else (i, other)
                pairs.append((i * count_y + j, target[0] * count_y + target[1]))
    return lax.ppermute(value, ("gx", "gy"), pairs)


def local(initial_temp, material, plate, cooling, principal, angles, aging_scale):
    depth, rows, width = initial_temp.shape
    sizes = (lax.axis_size("gx"), lax.axis_size("gy"))
    devices = sizes[0] * sizes[1]
    f32 = jnp.float32

    def shape(*dims):
        return jax.ShapeDtypeStruct(dims, f32)

    raw = jnp.concatenate([principal, angles, aging_scale[:, None]], axis=1).T
    raw = jnp.pad(raw, ((0, 1), (1, LANES - 1 - raw.shape[1])))
    own, send_a, send_b, pack, table = pl.pallas_call(
        pack_kernel,
        out_shape=(
            shape(3, rows, depth, LANES),
            shape(3, HALO, depth, LANES),
            shape(3, HALO, depth, LANES),
            shape(3, depth, LANES),
            shape(LINKS + 1, 8, LANES),
        ),
        in_specs=[VMEM] * 5,
        out_specs=(VMEM,) * 5,
        name="pack",
    )(initial_temp, material, plate, cooling, raw)

    side_b = swap(pack, sizes, 1, 1)
    side_a = swap(pack, sizes, 1, 0)
    got_b = swap(send_b, sizes, 0, 1)
    got_a = swap(send_a, sizes, 0, 0)
    even = lax.rem(lax.axis_index("gy"), 2) == 0
    lane = lane_of(pack.shape)
    from_left = lax.rem(lane, SLOT) < HALO
    mid = jnp.where(from_left == even, side_b, side_a)
    mid_b = swap(mid, sizes, 0, 1)
    mid_a = swap(mid, sizes, 0, 0)

    total_rows = rows + 2 * HALO
    ext, weights, diag, shifted, third, part = pl.pallas_call(
        front_kernel,
        out_shape=(
            shape(3, total_rows, 2, depth, LANES),
            shape(LINKS + 1, rows + 4, 2, DEPTH_PAD, LANES),
            shape(rows + 4, 2, depth, LANES),
            shape(3, 3, rows + 6, 2, DEPTH_PAD, LANES),
            shape(rows, depth, LANES),
            shape(devices, LANES),
        ),
        in_specs=[VMEM] * 7,
        out_specs=(VMEM,) * 6,
        scratch_shapes=[pltpu.VMEM((3, rows + 6, 2, DEPTH_PAD, LANES), f32)],
        name="front",
    )(own, got_a, got_b, mid, mid_a, mid_b, table)

    parts = lax.all_to_all(part, ("gx", "gy"), 0, 0, tiled=True)

    adjoint, sens = pl.pallas_call(
        back_kernel,
        out_shape=(shape(depth, rows, LANES), shape(depth, rows, LANES)),
        in_specs=[VMEM] * 6,
        out_specs=(VMEM,) * 2,
        scratch_shapes=[
            pltpu.VMEM((LINKS + 1, 6, 2, DEPTH_PAD, LANES), f32),
            pltpu.VMEM((6, 2, depth, LANES), f32),
            pltpu.VMEM((3, 10, 2, DEPTH_PAD, LANES), f32),
            pltpu.VMEM((3, 3, 6, 2, DEPTH_PAD, LANES), f32),
            pltpu.VMEM((rows + 6, 2, depth, LANES), f32),
            pltpu.VMEM((3, rows + 6, 2, DEPTH_PAD, LANES), f32),
        ],
        name="back",
    )(ext, weights, diag, shifted, third, table)

    scale = float(depth * rows * width * devices) / jnp.sum(parts)
    return adjoint * scale, sens * plate.astype(f32) * scale


def solution(mesh):
    block = P(None, "gx", "gy")
    return jax.shard_map(
        local,
        mesh=mesh,
        in_specs=(block, block, block, block, P(), P(), P()),
        out_specs=(block, block),
        check_vma=False,
    )
```

```python
import functools

import jax
import jax.numpy as jnp
from jax import lax
from jax.experimental import pallas as pl
from jax.experimental.pallas import tpu as pltpu
from jax.sharding import PartitionSpec as P

STEPS = 3
STEP_SCALE = 0.06
COOL_TEMP = 0.85
AGE_BETA = 8.0
HALF_OFFSETS = [
    (first, second, third)
    for first in (-1, 0, 1)
    for second in (-1, 0, 1)
    for third in (-1, 0, 1)
    if (first, second, third) > (0, 0, 0)
]
LINKS = len(HALF_OFFSETS)
HALO = 2 * STEPS
LANES = 128
SLOT = 16
T0, ID, COEFF = 0, 1, 2
VMEM = pl.BlockSpec(memory_space=pltpu.VMEM)
PAD = 8
GUARD = 8
PARTS = 7


def lane_of(shape):
    return lax.broadcasted_iota(jnp.int32, shape, len(shape) - 1)


def table_kernel(principal, angles, aging, table, line):
    count = aging.shape[1]
    line[...] = jnp.zeros_like(line)
    line[0:3, 0:count] = principal[...]
    line[3:6, 0:count] = angles[...]
    line[6:7, 0:count] = aging[...]
    raw = pltpu.roll(line[...], 1, 1)
    p = [raw[k : k + 1] for k in range(3)]
    cosine, sine = jnp.cos(raw[3:6]), jnp.sin(raw[3:6])
    c1, c2, c3 = cosine[0:1], cosine[1:2], cosine[2:3]
    s1, s2, s3 = sine[0:1], sine[1:2], sine[2:3]
    columns = [
        (c1 * c3 - s1 * c2 * s3, s1 * c3 + c1 * c2 * s3, s2 * s3),
        (-c1 * s3 - s1 * c2 * c3, -s1 * s3 + c1 * c2 * c3, s2 * c3),
        (s1 * s2, -c1 * s2, c2),
    ]
    rows = []
    for i, j, factor in ((0, 0, 1), (1, 1, 1), (2, 2, 1), (0, 1, 2), (0, 2, 2), (1, 2, 2)):
        total = sum(p[k] * (columns[k][i] * columns[k][j]) for k in range(3))
        rows.append(STEP_SCALE * factor * total)
    rows.append(raw[6:7])
    for k, row in enumerate(rows):
        table[k] = jnp.broadcast_to(row, (8, LANES))


def pack_kernel(temp, material, plate, cooling, own, send_a, send_b, pack):
    depth, rows, _ = temp.shape
    lane = lane_of((depth, LANES))
    packs = [jnp.zeros((depth, LANES), jnp.float32) for _ in range(3)]
    for x in range(rows):
        fields = (
            temp[:, x, :],
            (material[:, x, :] + 1).astype(jnp.float32),
            cooling[:, x, :] * plate[:, x, :].astype(jnp.float32),
        )
        mine = (lane >= SLOT * x) & (lane < SLOT * (x + 1))
        for f in range(3):
            own[f, x] = fields[f]
            moved = pltpu.roll(fields[f], (SLOT * x + HALO) % LANES, 1)
            packs[f] = jnp.where(mine, moved, packs[f])
    even = lax.rem(lax.axis_index("gx"), 2) == 0
    first_a = jnp.where(even, rows - HALO, 0)
    first_b = jnp.where(even, 0, rows - HALO)
    for f in range(3):
        pack[f] = packs[f]
        for r in range(HALO):
            send_a[f, r] = own[f, first_a + r]
            send_b[f, r] = own[f, first_b + r]


class Rows:
    def __init__(self):
        self.where = {}

    def flat(self, ref, rows, depth, pad, first_block=0, tiles=(0, 1)):
        block = first_block
        for r in rows:
            for t in tiles:
                start = block * (pad + depth) + (pad or GUARD)
                self.where[r, t] = (ref, None, start)
                block += 1
        return block

    def stacked(self, ref, rows, lead=(), first=0, tiles=(0, 1)):
        for r in rows:
            for t in tiles:
                self.where[r, t] = (ref, (*lead, r - first, t), 0)

    def of(self, r, t, depth, oz=0):
        ref, index, start = self.where[r, t]
        if index is None:
            return ref[pl.ds(start + oz, depth)]
        return ref[index]

    def put(self, r, t, value):
        ref, index, start = self.where[r, t]
        if index is None:
            ref[pl.ds(start, value.shape[0])] = value
        else:
            ref[index] = value


def clear_pads(ref, blocks, depth):
    zero = jnp.zeros((PAD, LANES), jnp.float32)
    for block in range(blocks + 1):
        ref[pl.ds(block * (PAD + depth), PAD)] = zero


def lane_shift(pair, by):
    lane = lane_of(pair[0].shape)
    moved = [pltpu.roll(value, (-by) % LANES, 1) for value in pair]
    edge = lane == (LANES - 1 if by > 0 else 0)
    return [jnp.where(edge, moved[1 - t], moved[t]) for t in (0, 1)]


def put_shifted(fields, r, pair):
    for by in (-1, 0, 1):
        moved = pair if by == 0 else lane_shift(pair, by)
        for t in (0, 1):
            fields[by].put(r, t, moved[t])


def near_sum(weights, fields, r, t, depth):
    total = None
    for k, (oz, ox, oy) in enumerate(HALF_OFFSETS):
        both = fields[oy].of(r + ox, t, depth, oz) + fields[-oy].of(r - ox, t, depth, -oz)
        term = weights[k].of(r, t, depth) * both
        total = term if total is None else total + term
    return total


def expand(table, weights, ids, rows, depth):
    tables = [table[k] for k in range(PARTS)]
    for r in rows:
        for t in (0, 1):
            index = ids.of(r, t, depth).astype(jnp.int32)
            halves = []
            for half in range(depth // 8):
                part = index[8 * half : 8 * half + 8]
                zz, xx, yy, zx, zy, xy, aging = (
                    jnp.take_along_axis(entry, part, axis=1, mode="promise_in_bounds")
                    for entry in tables
                )
                found = {(1, 0, 0): zz, (0, 1, 0): xx, (0, 0, 1): yy}
                for first, second, cross, one, two in (
                    (zz, xx, zx, (1, 1, 0), (1, -1, 0)),
                    (zz, yy, zy, (1, 0, 1), (1, 0, -1)),
                    (xx, yy, xy, (0, 1, 1), (0, 1, -1)),
                ):
                    mean = (first + second) * 0.25
                    cross = cross * 0.25
                    found[one], found[two] = mean + cross, mean - cross
                ninth = 1.0 / 9.0
                trace = (zz + xx + yy) * ninth
                zx, zy, xy = zx * ninth, zy * ninth, xy * ninth
                up, down = trace + zx, trace - zx
                plus, minus = zy + xy, zy - xy
                found[1, 1, 1], found[1, 1, -1] = up + plus, up - plus
                found[1, -1, 1], found[1, -1, -1] = down + minus, down - minus
                halves.append([found[offset] for offset in HALF_OFFSETS] + [aging])
            for k in range(LINKS + 1):
                weights[k].put(r, t, jnp.concatenate([half[k] for half in halves], axis=0))


def rate_of(state):
    good = state > 0.5
    inverse = 1.0 / jnp.where(good, state, 1.0)
    return jnp.where(good, jnp.exp(AGE_BETA * (1.0 - inverse)), 0.0), inverse


class Plan:
    def __init__(self, rows):
        self.rows = rows
        self.all = range(rows + 2 * HALO)

    def cone(self, radius):
        return range(HALO - radius, HALO + self.rows + radius)

    def ring(self, radius, inner):
        middle = self.cone(inner)
        return [r for r in self.cone(radius) if r not in middle]


def weight_rows(ref, rows, depth):
    weights, block = [], 0
    for _ in range(LINKS + 1):
        field = Rows()
        block = field.flat(ref, rows, depth, 0, block)
        weights.append(field)
    return weights


def shifted_rows(ref, rows, depth):
    fields, block = {}, 0
    for oy in (-1, 0, 1):
        fields[oy] = Rows()
        block = fields[oy].flat(ref, rows, depth, PAD, block)
    clear_pads(ref, block, depth)
    return fields


def padded_size(blocks, depth):
    return (blocks * (PAD + depth) + PAD, LANES)


def guarded_size(blocks, depth):
    return (blocks * depth + 2 * GUARD, LANES)


def validity(ids, r, depth):
    return [jnp.where(ids.of(r, t, depth) > 0.5, 1.0, 0.0) for t in (0, 1)]


def front_kernel(
    own, got_a, got_b, mid, mid_a, mid_b, table,
    ext, keep_ref, first_ref, second_ref, third_ref, part,
    weights_ref, even_ref, odd_ref,
):
    _, rows, depth, _ = own.shape
    plan = Plan(rows)
    even = lax.rem(lax.axis_index("gx"), 2) == 0
    base_a = jnp.where(even, HALO + rows, 0)
    base_b = jnp.where(even, 0, HALO + rows)
    lane = lane_of((depth, LANES))
    halo_lane = (lane < HALO) | (lane >= LANES - HALO)
    for f in range(3):
        for r in range(HALO):
            ext[f, base_a + r, 0] = got_a[f, r]
            ext[f, base_b + r, 0] = got_b[f, r]
        for x in range(rows):
            ext[f, HALO + x, 0] = own[f, x]
        low = jnp.where(even, mid_b[f], mid_a[f])
        high = jnp.where(even, mid_a[f], mid_b[f])
        for r in plan.all:
            x = r - HALO
            source, x = (
                (low, x + rows) if x < 0 else (high, x - rows) if x >= rows else (mid[f], x)
            )
            moved = pltpu.roll(source, (-(SLOT * x + HALO)) % LANES, 1)
            ext[f, r, 1] = jnp.where(halo_lane, moved, 0.0)

    temp, ids, coeff = Rows(), Rows(), Rows()
    for field, f in ((temp, T0), (ids, ID), (coeff, COEFF)):
        field.stacked(ext, plan.all, (f,))
    weights = weight_rows(weights_ref, plan.cone(2), depth)
    keep = Rows()
    keep.stacked(keep_ref, plan.cone(2), (), HALO - 2)
    shifted = [shifted_rows(ref, plan.cone(3), depth) for ref in (even_ref, odd_ref)]
    expand(table, weights, ids, plan.cone(2), depth)
    for r in plan.cone(3):
        put_shifted(shifted[1], r, validity(ids, r, depth))
        put_shifted(shifted[0], r, [temp.of(r, t, depth) for t in (0, 1)])
    for r in plan.cone(2):
        for t in (0, 1):
            diag = coeff.of(r, t, depth) + near_sum(weights, shifted[1], r, t, depth)
            keep.put(r, t, 1.0 - diag)
    loss = jnp.zeros((depth, LANES), jnp.float32)
    for n in range(STEPS):
        source = shifted[n % 2]
        for r in plan.cone(2 - n):
            pair = []
            for t in (0, 1) if n < 2 else (0,):
                center = source[0].of(r, t, depth)
                near = near_sum(weights, source, r, t, depth)
                pair.append(keep.of(r, t, depth) * center + near + coeff.of(r, t, depth) * COOL_TEMP)
            if n < 2:
                put_shifted(shifted[(n + 1) % 2], r, pair)
                for t in (0, 1):
                    (first_ref, second_ref)[n][r - HALO + 2 - n, t] = pair[t]
            else:
                third_ref[r - HALO] = pair[0]
            if HALO <= r < HALO + rows:
                rate, _ = rate_of(pair[0])
                loss = loss + weights[LINKS].of(r, 0, depth) * rate
    part[...] = jnp.broadcast_to(jnp.sum(loss, axis=0, keepdims=True), part.shape)


def back_kernel(
    ext, keep_in, first_in, second_in, third_in, table, plate,
    adjoint_out, sens_out,
    weights_ref, keep_ref, valid_ref, states_ref, third_ref, adjoint_ref,
):
    rows, depth, _ = third_in.shape
    plan = Plan(rows)
    temp, ids, coeff = Rows(), Rows(), Rows()
    for field, f in ((temp, T0), (ids, ID), (coeff, COEFF)):
        field.stacked(ext, plan.all, (f,))
    outer = plan.ring(5, 2)
    for start in (0, weights_ref.shape[0] - GUARD):
        weights_ref[pl.ds(start, GUARD)] = jnp.zeros((GUARD, LANES), jnp.float32)
    weights = weight_rows(weights_ref, plan.cone(5), depth)
    keep = Rows()
    keep.stacked(keep_in, plan.cone(2), (), HALO - 2)
    for i, r in enumerate(outer):
        for t in (0, 1):
            keep.where[r, t] = (keep_ref, (i, t), 0)
    valid_list = [r for r in plan.all if r not in plan.cone(1)]
    valid = shifted_rows(valid_ref, valid_list, depth)
    shifted, block = [{}, {}, {}], 0
    for n in range(3):
        held = plan.ring(6 - n, 1 - n) if n < 2 else plan.cone(4)
        for oy in (-1, 0, 1):
            shifted[n][oy] = Rows()
            block = shifted[n][oy].flat(states_ref, held, depth, PAD, block)
    clear_pads(states_ref, block, depth)

    expand(table, weights, ids, plan.cone(5), depth)
    for r in valid_list:
        put_shifted(valid, r, validity(ids, r, depth))
    for r in plan.ring(6, 1):
        put_shifted(shifted[0], r, [temp.of(r, t, depth) for t in (0, 1)])
    for r in plan.ring(2, 0):
        put_shifted(shifted[1], r, [first_in[r - HALO + 2, t] for t in (0, 1)])
    for r in plan.cone(1):
        put_shifted(shifted[2], r, [second_in[r - HALO + 1, t] for t in (0, 1)])
    for r in outer:
        for t in (0, 1):
            diag = coeff.of(r, t, depth) + near_sum(weights, valid, r, t, depth)
            keep.put(r, t, 1.0 - diag)
    states = [temp, Rows(), shifted[2][0], Rows()]
    states[1].stacked(first_in, plan.cone(2), (), HALO - 2)
    states[3].stacked(third_ref, plan.cone(3), (), HALO - 3)
    for r in plan.cone(0):
        states[3].where[r, 0] = (third_in, (r - HALO,), 0)
    for n in range(STEPS):
        todo = [(r, t) for r in plan.ring(5 - n, 2 - n) for t in (0, 1)]
        if n == 2:
            todo = todo + [(r, 1) for r in plan.cone(0)]
        pair = {}
        for r, t in todo:
            center = shifted[n][0].of(r, t, depth)
            near = near_sum(weights, shifted[n], r, t, depth)
            value = keep.of(r, t, depth) * center + near + coeff.of(r, t, depth) * COOL_TEMP
            if n == 2:
                states[3].put(r, t, value)
                continue
            pair[t] = value
            if t == 1:
                put_shifted(shifted[n + 1], r, [pair[0], pair[1]])

    def drive(n, r, t):
        rate, inverse = rate_of(states[n].of(r, t, depth))
        return weights[LINKS].of(r, t, depth) * AGE_BETA * rate * (inverse * inverse)

    vectors, block = [], 0
    for n in range(3):
        vectors.append(Rows())
        block = vectors[n].flat(adjoint_ref, plan.cone(3 - n), depth, PAD, block)
    clear_pads(adjoint_ref, block, depth)
    for r in plan.cone(3):
        for t in (0, 1):
            vectors[0].put(r, t, drive(3, r, t))
    for n in range(3):
        vector = vectors[n]
        sums = {}
        for source in plan.cone(3 - n):
            for t in (0, 1):
                reads = {oz: vector.of(source, t, depth, -oz) for oz in (-1, 0, 1)}
                for k, offset in enumerate(HALF_OFFSETS):
                    product = {}
                    for sign in (1, -1):
                        oz, ox, oy = (sign * o for o in offset)
                        target = source + ox
                        if oz not in product:
                            product[oz] = reads[oz] * weights[k].of(source, t, depth, -oz)
                        if target in plan.cone(2 - n):
                            key = (target, oy, t)
                            sums[key] = sums[key] + product[oz] if key in sums else product[oz]
            target = source - 1
            if target not in plan.cone(2 - n):
                continue
            plus = lane_shift([sums.pop((target, 1, t)) for t in (0, 1)], -1)
            minus = lane_shift([sums.pop((target, -1, t)) for t in (0, 1)], 1)
            for t in (0, 1) if n < 2 else (0,):
                result = (
                    keep.of(target, t, depth) * vector.of(target, t, depth)
                    + sums.pop((target, 0, t))
                    + (plus[t] + minus[t])
                )
                if n < 2:
                    vectors[n + 1].put(target, t, result + drive(2 - n, target, t))
                else:
                    adjoint_out[:, target - HALO, :] = result
    for r in plan.cone(0):
        total = None
        for n in range(3):
            term = vectors[2 - n].of(r, 0, depth) * (states[n].of(r, 0, depth) - COOL_TEMP)
            total = term if total is None else total + term
        sens_out[:, r - HALO, :] = -total * plate[:, r - HALO, :].astype(jnp.float32)


def scale_kernel(cells, parts, adjoint, sens, adjoint_out, sens_out):
    row = jnp.sum(parts[...], axis=0, keepdims=True)
    scale = cells / jnp.sum(row, axis=1, keepdims=True)
    adjoint_out[...] = adjoint[...] * scale.reshape(1, 1, 1)
    sens_out[...] = sens[...] * scale.reshape(1, 1, 1)


def pairing(count, first):
    out = {}
    for i in range(first, count - 1, 2):
        out[i], out[i + 1] = i + 1, i
    return out


def swap(value, sizes, axis, first):
    count_x, count_y = sizes
    partner = pairing(sizes[axis], first)
    pairs = []
    for i in range(count_x):
        for j in range(count_y):
            other = partner.get((i, j)[axis])
            if other is not None:
                target = (other, j) if axis == 0 else (i, other)
                pairs.append((i * count_y + j, target[0] * count_y + target[1]))
    return lax.ppermute(value, ("gx", "gy"), pairs)


def local(initial_temp, material, plate, cooling, principal, angles, aging_scale):
    depth, rows, width = initial_temp.shape
    sizes = (lax.axis_size("gx"), lax.axis_size("gy"))
    devices = sizes[0] * sizes[1]
    f32 = jnp.float32

    def shape(*dims):
        return jax.ShapeDtypeStruct(dims, f32)

    def call(kernel, name, mib, out_shape, scratch=()):
        return pl.pallas_call(
            kernel,
            out_shape=out_shape,
            scratch_shapes=[pltpu.VMEM(dims, f32) for dims in scratch],
            name=name,
            compiler_params=pltpu.CompilerParams(vmem_limit_bytes=mib * 2**20),
        )

    own, send_a, send_b, pack = call(
        pack_kernel,
        "pack",
        2,
        (
            shape(3, rows, depth, LANES),
            shape(3, HALO, depth, LANES),
            shape(3, HALO, depth, LANES),
            shape(3, depth, LANES),
        ),
    )(initial_temp, material, plate, cooling)
    side_b = swap(pack, sizes, 1, 1)
    side_a = swap(pack, sizes, 1, 0)
    got_b = swap(send_b, sizes, 0, 1)
    got_a = swap(send_a, sizes, 0, 0)
    table = call(table_kernel, "table", 2, shape(PARTS, 8, LANES), ((8, LANES),))(
        principal.T, angles.T, aging_scale[None]
    )
    even = lax.rem(lax.axis_index("gy"), 2) == 0
    from_left = lax.rem(lane_of(pack.shape), SLOT) < HALO
    mid = jnp.where(from_left == even, side_b, side_a)
    mid_b = swap(mid, sizes, 0, 1)
    mid_a = swap(mid, sizes, 0, 0)

    total_rows = rows + 2 * HALO
    pairs = 2 * rows
    ext, keep, first, second, third, part = call(
        front_kernel,
        "front",
        20,
        (
            shape(3, total_rows, 2, depth, LANES),
            shape(rows + 4, 2, depth, LANES),
            shape(rows + 4, 2, depth, LANES),
            shape(rows + 2, 2, depth, LANES),
            shape(rows, depth, LANES),
            shape(devices, LANES),
        ),
        (
            guarded_size((LINKS + 1) * (pairs + 8), depth),
            padded_size(3 * (pairs + 12), depth),
            padded_size(3 * (pairs + 12), depth),
        ),
    )(own, got_a, got_b, mid, mid_a, mid_b, table)
    parts = lax.all_to_all(part, ("gx", "gy"), 0, 0, tiled=True)
    adjoint, sens = call(
        back_kernel,
        "back",
        24,
        (shape(depth, rows, LANES), shape(depth, rows, LANES)),
        (
            guarded_size((LINKS + 1) * (pairs + 20), depth),
            (6, 2, depth, LANES),
            padded_size(3 * 2 * 10, depth),
            padded_size(3 * (2 * 10 + 2 * 10 + pairs + 16), depth),
            (rows + 6, 2, depth, LANES),
            padded_size(3 * pairs + 4 * (3 + 2 + 1), depth),
        ),
    )(ext, keep, first, second, third, table, plate)
    return call(
        functools.partial(scale_kernel, float(depth * rows * width * devices)),
        "scale",
        2,
        (shape(depth, rows, LANES), shape(depth, rows, LANES)),
    )(parts, adjoint, sens)


def solution(mesh):
    block = P(None, "gx", "gy")
    return jax.shard_map(
        local,
        mesh=mesh,
        in_specs=(block, block, block, block, P(), P(), P()),
        out_specs=(block, block),
        check_vma=False,
    )
```

```python
import functools

import jax
import jax.numpy as jnp
from jax import lax
from jax.experimental import pallas as pl
from jax.experimental.pallas import tpu as pltpu
from jax.sharding import PartitionSpec as P

STEPS = 3
STEP_SCALE = 0.06
COOL_TEMP = 0.85
AGE_BETA = 8.0
HALF_OFFSETS = [
    (first, second, third)
    for first in (-1, 0, 1)
    for second in (-1, 0, 1)
    for third in (-1, 0, 1)
    if (first, second, third) > (0, 0, 0)
]
LINKS = len(HALF_OFFSETS)
HALO = 2 * STEPS
LANES = 128
SLOT = 16
T0, ID, COEFF = 0, 1, 2
VMEM = pl.BlockSpec(memory_space=pltpu.VMEM)
PAD = 8
GUARD = 8
PARTS = 7


def lane_of(shape):
    return lax.broadcasted_iota(jnp.int32, shape, len(shape) - 1)


def table_kernel(principal, angles, aging, table, line):
    count = aging.shape[1]
    line[...] = jnp.zeros_like(line)
    line[0:3, 0:count] = principal[...]
    line[3:6, 0:count] = angles[...]
    line[6:7, 0:count] = aging[...]
    raw = pltpu.roll(line[...], 1, 1)
    p = [raw[k : k + 1] for k in range(3)]
    cosine, sine = jnp.cos(raw[3:6]), jnp.sin(raw[3:6])
    c1, c2, c3 = cosine[0:1], cosine[1:2], cosine[2:3]
    s1, s2, s3 = sine[0:1], sine[1:2], sine[2:3]
    columns = [
        (c1 * c3 - s1 * c2 * s3, s1 * c3 + c1 * c2 * s3, s2 * s3),
        (-c1 * s3 - s1 * c2 * c3, -s1 * s3 + c1 * c2 * c3, s2 * c3),
        (s1 * s2, -c1 * s2, c2),
    ]
    rows = []
    for i, j, factor in ((0, 0, 1), (1, 1, 1), (2, 2, 1), (0, 1, 2), (0, 2, 2), (1, 2, 2)):
        total = sum(p[k] * (columns[k][i] * columns[k][j]) for k in range(3))
        rows.append(STEP_SCALE * factor * total)
    rows.append(raw[6:7])
    for k, row in enumerate(rows):
        table[k] = jnp.broadcast_to(row, (8, LANES))


def pack_kernel(temp_in, material_in, plate_in, cooling_in, own, pack, temp, material, plate, cooling, sems):
    copies = [
        pltpu.make_async_copy(source, target, sems.at[i])
        for i, (source, target) in enumerate(
            ((temp_in, temp), (material_in, material), (plate_in, plate), (cooling_in, cooling))
        )
    ]
    for copy in copies:
        copy.start()
    for copy in copies:
        copy.wait()
    depth, rows, _ = temp.shape
    lane = lane_of((depth, LANES))
    packs = [jnp.zeros((depth, LANES), jnp.float32) for _ in range(3)]
    for x in range(rows):
        fields = (
            temp[:, x, :],
            (material[:, x, :] + 1).astype(jnp.float32),
            cooling[:, x, :] * plate[:, x, :].astype(jnp.float32),
        )
        mine = (lane >= SLOT * x) & (lane < SLOT * (x + 1))
        for f in range(3):
            own[f, x] = fields[f]
            moved = pltpu.roll(fields[f], (SLOT * x + HALO) % LANES, 1)
            packs[f] = jnp.where(mine, moved, packs[f])
    for f in range(3):
        pack[f] = packs[f]


def middle_kernel(last_y, own, side_a, side_b, mid, send_a, send_b):
    _, rows, depth, _ = own.shape
    at_y = lax.axis_index("gy")
    even_y = lax.rem(at_y, 2) == 0
    even_x = lax.rem(lax.axis_index("gx"), 2) == 0
    from_left = lax.rem(lane_of((depth, LANES)), SLOT) < HALO
    for f in range(3):
        left = jnp.where(at_y == 0, 0.0, jnp.where(even_y, side_b[f], side_a[f]))
        right = jnp.where(at_y == last_y, 0.0, jnp.where(even_y, side_a[f], side_b[f]))
        value = jnp.where(from_left, left, right)
        mid[f] = value
        send_a[f, HALO] = value
        send_b[f, HALO] = value
    first_a = jnp.where(even_x, rows - HALO, 0)
    first_b = jnp.where(even_x, 0, rows - HALO)
    for f in range(3):
        for r in range(HALO):
            send_a[f, r] = own[f, first_a + r]
            send_b[f, r] = own[f, first_b + r]


class Rows:
    def __init__(self):
        self.where = {}

    def flat(self, ref, rows, depth, pad, first_block=0, tiles=(0, 1)):
        block = first_block
        for r in rows:
            for t in tiles:
                start = block * (pad + depth) + (pad or GUARD)
                self.where[r, t] = (ref, None, start)
                block += 1
        return block

    def stacked(self, ref, rows, lead=(), first=0, tiles=(0, 1)):
        for r in rows:
            for t in tiles:
                self.where[r, t] = (ref, (*lead, r - first, t), 0)

    def of(self, r, t, size, offset=0):
        ref, index, start = self.where[r, t]
        if index is None:
            return ref[pl.ds(start + offset, size)]
        return ref[(*index, pl.ds(offset, size))]

    def put(self, r, t, value, offset=0):
        ref, index, start = self.where[r, t]
        if index is None:
            ref[pl.ds(start + offset, value.shape[0])] = value
        else:
            ref[(*index, pl.ds(offset, value.shape[0]))] = value


def clear_pads(ref, blocks, depth):
    zero = jnp.zeros((PAD, LANES), jnp.float32)
    for block in range(blocks + 1):
        ref[pl.ds(block * (PAD + depth), PAD)] = zero


def lane_shift(pair, by):
    lane = lane_of(pair[0].shape)
    moved = [pltpu.roll(value, (-by) % LANES, 1) for value in pair]
    edge = lane == (LANES - 1 if by > 0 else 0)
    return [jnp.where(edge, moved[1 - t], moved[t]) for t in (0, 1)]


def put_shifted(fields, r, pair):
    for by in (-1, 0, 1):
        moved = pair if by == 0 else lane_shift(pair, by)
        for t in (0, 1):
            fields[by].put(r, t, moved[t])


def advance(weights, keep, coeff, fields, rows, tiles, depth, done):
    for t in tiles:
        for half in range(depth // 8):
            base = 8 * half
            window = {}
            for r in rows:
                for other in (r - 1, r, r + 1):
                    if other not in window:
                        window[other] = {
                            (oz, oy): fields[oy].of(other, t, 8, base + oz)
                            for oz in (-1, 0, 1)
                            for oy in (-1, 0, 1)
                        }
                total = coeff.of(r, t, 8, base) * COOL_TEMP
                total = total + keep.of(r, t, 8, base) * window[r][0, 0]
                for k, (oz, ox, oy) in enumerate(HALF_OFFSETS):
                    both = window[r + ox][oz, oy] + window[r - ox][-oz, -oy]
                    total = total + weights[k].of(r, t, 8, base) * both
                done(r, t, base, total)
                window.pop(r - 1)


def reach(at, size):
    above = jnp.where(at < size - 1, 1.0, 0.0)
    below = jnp.where(at > 0, 1.0, 0.0)
    return above + below, above - below


def expand(table, weights, keep, ids, coeff, rows, grid, own_rows, depth):
    tables = [table[k] for k in range(PARTS)]
    quarter, ninth = 0.25, 1.0 / 9.0
    lane = lane_of((8, LANES))
    first_y = lax.axis_index("gy") * LANES
    first_x = lax.axis_index("gx") * own_rows - HALO
    for t in (0, 1):
        y = first_y + (lane if t == 0 else jnp.where(lane < LANES // 2, lane + LANES, lane - LANES))
        sum_y, dif_y = reach(y, grid[1])
        for half in range(depth // 8):
            z = lax.broadcasted_iota(jnp.int32, (8, LANES), 0) + 8 * half
            sum_z, dif_z = reach(z, depth)
            zz_0, zz_1 = sum_z * (1.0 + quarter * sum_y), sum_z * (quarter + ninth * sum_y)
            yy_0, yy_1 = sum_y * (1.0 + quarter * sum_z), sum_y * (quarter + ninth * sum_z)
            xx_1 = 1.0 + quarter * (sum_z + sum_y) + ninth * sum_z * sum_y
            zx_1 = dif_z * (quarter + ninth * sum_y)
            xy_1 = dif_y * (quarter + ninth * sum_z)
            zy_0, zy_1 = quarter * dif_z * dif_y, ninth * dif_z * dif_y
            for r in rows:
                sum_x, dif_x = reach(first_x + r, grid[0])
                part = ids.of(r, t, 8, 8 * half).astype(jnp.int32)
                zz, xx, yy, zx, zy, xy, aging = (
                    jnp.take_along_axis(entry, part, axis=1, mode="promise_in_bounds")
                    for entry in tables
                )
                near = (
                    zz * (zz_0 + sum_x * zz_1)
                    + yy * (yy_0 + sum_x * yy_1)
                    + zy * (zy_0 + sum_x * zy_1)
                    + xx * (sum_x * xx_1)
                    + dif_x * (zx * zx_1 + xy * xy_1)
                )
                keep.put(r, t, 1.0 - (coeff.of(r, t, 8, 8 * half) + near), 8 * half)
                found = {(1, 0, 0): zz, (0, 1, 0): xx, (0, 0, 1): yy}
                for first, second, cross, one, two in (
                    (zz, xx, zx, (1, 1, 0), (1, -1, 0)),
                    (zz, yy, zy, (1, 0, 1), (1, 0, -1)),
                    (xx, yy, xy, (0, 1, 1), (0, 1, -1)),
                ):
                    mean = (first + second) * quarter
                    cross = cross * quarter
                    found[one], found[two] = mean + cross, mean - cross
                trace = (zz + xx + yy) * ninth
                zx, zy, xy = zx * ninth, zy * ninth, xy * ninth
                up, down = trace + zx, trace - zx
                plus, minus = zy + xy, zy - xy
                found[1, 1, 1], found[1, 1, -1] = up + plus, up - plus
                found[1, -1, 1], found[1, -1, -1] = down + minus, down - minus
                for k, offset in enumerate(HALF_OFFSETS):
                    weights[k].put(r, t, found[offset], 8 * half)
                weights[LINKS].put(r, t, aging, 8 * half)


def rate_of(state):
    good = state > 0.5
    inverse = 1.0 / jnp.where(good, state, 1.0)
    return jnp.where(good, jnp.exp(AGE_BETA * (1.0 - inverse)), 0.0), inverse


class Plan:
    def __init__(self, rows):
        self.rows = rows
        self.all = range(rows + 2 * HALO)

    def cone(self, radius):
        return range(HALO - radius, HALO + self.rows + radius)

    def ring(self, radius, inner):
        middle = self.cone(inner)
        return [r for r in self.cone(radius) if r not in middle]


def weight_rows(ref, rows, depth):
    weights, block = [], 0
    for _ in range(LINKS + 1):
        field = Rows()
        block = field.flat(ref, rows, depth, 0, block)
        weights.append(field)
    return weights


def shifted_rows(ref, rows, depth):
    fields, block = {}, 0
    for oy in (-1, 0, 1):
        fields[oy] = Rows()
        block = fields[oy].flat(ref, rows, depth, PAD, block)
    clear_pads(ref, block, depth)
    return fields


def padded_size(blocks, depth):
    return (blocks * (PAD + depth) + PAD, LANES)


def guarded_size(blocks, depth):
    return (blocks * depth + 2 * GUARD, LANES)


def front_kernel(
    grid, own, mid, got_a, got_b, table,
    ext, first_ref, second_ref, third_ref, part,
    weights_ref, keep_ref, even_ref, odd_ref,
):
    _, rows, depth, _ = own.shape
    plan = Plan(rows)
    even = lax.rem(lax.axis_index("gx"), 2) == 0
    base_a = jnp.where(even, HALO + rows, 0)
    base_b = jnp.where(even, 0, HALO + rows)
    lane = lane_of((depth, LANES))
    halo_lane = (lane < HALO) | (lane >= LANES - HALO)
    for f in range(3):
        for r in range(HALO):
            ext[f, base_a + r, 0] = got_a[f, r]
            ext[f, base_b + r, 0] = got_b[f, r]
        for x in range(rows):
            ext[f, HALO + x, 0] = own[f, x]
        low = jnp.where(even, got_b[f, HALO], got_a[f, HALO])
        high = jnp.where(even, got_a[f, HALO], got_b[f, HALO])
        for r in plan.all:
            x = r - HALO
            source, x = (
                (low, x + rows) if x < 0 else (high, x - rows) if x >= rows else (mid[f], x)
            )
            moved = pltpu.roll(source, (-(SLOT * x + HALO)) % LANES, 1)
            ext[f, r, 1] = jnp.where(halo_lane, moved, 0.0)

    temp, ids, coeff = Rows(), Rows(), Rows()
    for field, f in ((temp, T0), (ids, ID), (coeff, COEFF)):
        field.stacked(ext, plan.all, (f,))
    weights = weight_rows(weights_ref, plan.cone(2), depth)
    keep = Rows()
    keep.stacked(keep_ref, plan.cone(2), (), HALO - 2)
    shifted = [shifted_rows(ref, plan.cone(3), depth) for ref in (even_ref, odd_ref)]
    expand(table, weights, keep, ids, coeff, plan.cone(2), grid, rows, depth)
    for r in plan.cone(3):
        put_shifted(shifted[0], r, [temp.of(r, t, depth) for t in (0, 1)])
    losses = []
    for n in range(STEPS):
        out = Rows()
        out.stacked((first_ref, second_ref, third_ref)[n], plan.cone(2 - n), (), HALO - 2 + n)

        def done(r, t, base, value):
            out.put(r, t, value, base)
            if t == 0 and HALO <= r < HALO + rows:
                rate, _ = rate_of(value)
                losses.append(weights[LINKS].of(r, 0, 8, base) * rate)

        tiles = (0, 1) if n < 2 else (0,)
        advance(weights, keep, coeff, shifted[n % 2], plan.cone(2 - n), tiles, depth, done)
        if n < 2:
            for r in plan.cone(2 - n):
                put_shifted(shifted[(n + 1) % 2], r, [out.of(r, t, depth) for t in (0, 1)])
    loss = losses[0]
    for term in losses[1:]:
        loss = loss + term
    part[...] = jnp.broadcast_to(jnp.sum(loss, axis=0, keepdims=True), part.shape)


def back_kernel(
    grid, ext, first_in, second_in, third_in, table, plate,
    adjoint_out, sens_out,
    weights_ref, keep_ref, states_ref, third_ref, adjoint_ref, sums_ref, drive_ref,
):
    rows, _, depth, _ = third_in.shape
    plan = Plan(rows)
    temp, ids, coeff = Rows(), Rows(), Rows()
    for field, f in ((temp, T0), (ids, ID), (coeff, COEFF)):
        field.stacked(ext, plan.all, (f,))
    for start in (0, weights_ref.shape[0] - GUARD):
        weights_ref[pl.ds(start, GUARD)] = jnp.zeros((GUARD, LANES), jnp.float32)
    weights = weight_rows(weights_ref, plan.cone(5), depth)
    keep = Rows()
    keep.stacked(keep_ref, plan.cone(5), (), HALO - 5)
    shifted, block = [{}, {}, {}], 0
    for n in range(3):
        held = plan.ring(6 - n, 1 - n) if n < 2 else plan.cone(4)
        for oy in (-1, 0, 1):
            shifted[n][oy] = Rows()
            block = shifted[n][oy].flat(states_ref, held, depth, PAD, block)
    clear_pads(states_ref, block, depth)

    expand(table, weights, keep, ids, coeff, plan.cone(5), grid, rows, depth)
    for r in plan.ring(6, 1):
        put_shifted(shifted[0], r, [temp.of(r, t, depth) for t in (0, 1)])
    for r in plan.ring(2, 0):
        put_shifted(shifted[1], r, [first_in[r - HALO + 2, t] for t in (0, 1)])
    for r in plan.cone(1):
        put_shifted(shifted[2], r, [second_in[r - HALO + 1, t] for t in (0, 1)])
    states = [temp, Rows(), shifted[2][0], Rows()]
    states[1].stacked(first_in, plan.cone(2), (), HALO - 2)
    states[3].stacked(third_ref, plan.cone(3), (), HALO - 3)
    for n in range(STEPS):
        fresh = plan.ring(5 - n, 2 - n)
        low, high = [r for r in fresh if r < HALO], [r for r in fresh if r >= HALO]
        out = states[3] if n == 2 else shifted[n + 1][0]

        def done(r, t, base, value):
            out.put(r, t, value, base)

        for part in (low, high):
            advance(weights, keep, coeff, shifted[n], part, (0, 1), depth, done)
        if n == 2:
            advance(weights, keep, coeff, shifted[n], plan.cone(0), (1,), depth, done)
            continue
        for r in fresh:
            pair = [out.of(r, t, depth) for t in (0, 1)]
            for by in (-1, 1):
                moved = lane_shift(pair, by)
                for t in (0, 1):
                    shifted[n + 1][by].put(r, t, moved[t])
    for r in plan.cone(0):
        states[3].where[r, 0] = (third_in, (r - HALO, 0), 0)

    vectors, block = [], 0
    for n in range(3):
        vectors.append(Rows())
        block = vectors[n].flat(adjoint_ref, plan.cone(3 - n), depth, PAD, block)
    clear_pads(adjoint_ref, block, depth)
    drives = [None, Rows(), Rows(), vectors[0]]
    drives[1].stacked(drive_ref, plan.cone(1), (0,), HALO - 2)
    drives[2].stacked(drive_ref, plan.cone(2), (1,), HALO - 2)
    for n in range(1, 4):
        for r in plan.cone(n):
            for t in (0, 1):
                rate, inverse = rate_of(states[n].of(r, t, depth))
                factor = weights[LINKS].of(r, t, depth) * AGE_BETA
                drives[n].put(r, t, factor * rate * (inverse * inverse))
    sums = {}
    for oy in (-1, 0, 1):
        sums[oy] = Rows()
        sums[oy].stacked(sums_ref, plan.cone(2), (oy + 1,), HALO - 2)
    for n in range(3):
        vector = vectors[n]
        targets = plan.cone(2 - n)
        for t in (0, 1):
            for half in range(depth // 8):
                base = 8 * half
                totals = {}
                for source in plan.cone(3 - n):
                    reads = {oz: vector.of(source, t, 8, base - oz) for oz in (-1, 0, 1)}
                    for k, offset in enumerate(HALF_OFFSETS):
                        product = {}
                        for sign in (1, -1):
                            oz, ox, oy = (sign * o for o in offset)
                            if oz not in product:
                                weight = weights[k].of(source, t, 8, base - oz)
                                product[oz] = reads[oz] * weight
                            key = (source + ox, oy)
                            if key[0] in targets:
                                totals[key] = (
                                    totals[key] + product[oz] if key in totals else product[oz]
                                )
                    if source - 1 in targets:
                        for oy in (-1, 0, 1):
                            sums[oy].put(source - 1, t, totals.pop((source - 1, oy)), base)
        for r in targets:
            plus = lane_shift([sums[1].of(r, t, depth) for t in (0, 1)], -1)
            minus = lane_shift([sums[-1].of(r, t, depth) for t in (0, 1)], 1)
            for t in (0, 1) if n < 2 else (0,):
                result = (
                    keep.of(r, t, depth) * vector.of(r, t, depth)
                    + sums[0].of(r, t, depth)
                    + (plus[t] + minus[t])
                )
                if n < 2:
                    vectors[n + 1].put(r, t, result + drives[2 - n].of(r, t, depth))
                else:
                    adjoint_out[:, r - HALO, :] = result
    for r in plan.cone(0):
        total = None
        for n in range(3):
            term = vectors[2 - n].of(r, 0, depth) * (states[n].of(r, 0, depth) - COOL_TEMP)
            total = term if total is None else total + term
        sens_out[:, r - HALO, :] = -total * plate[:, r - HALO, :].astype(jnp.float32)


def scale_kernel(cells, parts, adjoint, sens, adjoint_out, sens_out):
    row = jnp.sum(parts[...], axis=0, keepdims=True)
    scale = cells / jnp.sum(row, axis=1, keepdims=True)
    adjoint_out[...] = adjoint[...] * scale.reshape(1, 1, 1)
    sens_out[...] = sens[...] * scale.reshape(1, 1, 1)


def pairing(count, first, ring):
    out = {}
    for i in range(first, count - 1, 2):
        out[i], out[i + 1] = i + 1, i
    if ring and 0 not in out:
        out[0], out[count - 1] = count - 1, 0
    return out


def swap(value, sizes, axis, first, ring=False):
    count_x, count_y = sizes
    partner = pairing(sizes[axis], first, ring)
    pairs = []
    for i in range(count_x):
        for j in range(count_y):
            other = partner.get((i, j)[axis])
            if other is not None:
                target = (other, j) if axis == 0 else (i, other)
                pairs.append((i * count_y + j, target[0] * count_y + target[1]))
    return lax.ppermute(value, ("gx", "gy"), pairs)


def local(initial_temp, material, plate, cooling, principal, angles, aging_scale):
    depth, rows, width = initial_temp.shape
    sizes = (lax.axis_size("gx"), lax.axis_size("gy"))
    devices = sizes[0] * sizes[1]
    f32 = jnp.float32

    def shape(*dims):
        return jax.ShapeDtypeStruct(dims, f32)

    def call(kernel, name, mib, out_shape, scratch=(), **specs):
        return pl.pallas_call(
            kernel,
            out_shape=out_shape,
            scratch_shapes=[
                pltpu.VMEM(dims, f32) if isinstance(dims, tuple) else dims for dims in scratch
            ],
            name=name,
            compiler_params=pltpu.CompilerParams(vmem_limit_bytes=mib * 2**20),
            **specs,
        )

    block = (depth, rows, LANES)
    own, pack = call(
        pack_kernel,
        "pack",
        2,
        (shape(3, rows, depth, LANES), shape(3, depth, LANES)),
        (
            block,
            pltpu.VMEM(block, jnp.int32),
            pltpu.VMEM(block, jnp.int32),
            block,
            pltpu.SemaphoreType.DMA((4,)),
        ),
        in_specs=[pl.BlockSpec(memory_space=pltpu.HBM)] * 4,
    )(*(pltpu.with_memory_space_constraint(x, pltpu.HBM) for x in (initial_temp, material, plate, cooling)))
    side_b = swap(pack, sizes, 1, 1, True)
    side_a = swap(pack, sizes, 1, 0)
    mid, send_a, send_b = call(
        functools.partial(middle_kernel, sizes[1] - 1),
        "middle",
        2,
        (
            shape(3, depth, LANES),
            shape(3, HALO + 1, depth, LANES),
            shape(3, HALO + 1, depth, LANES),
        ),
    )(own, side_a, side_b)
    got_b = swap(send_b, sizes, 0, 1)
    got_a = swap(send_a, sizes, 0, 0)
    table = call(table_kernel, "table", 2, shape(PARTS, 8, LANES), ((8, LANES),))(
        principal.T, angles.T, aging_scale[None]
    )

    total_rows = rows + 2 * HALO
    pairs = 2 * rows
    grid = (rows * sizes[0], width * sizes[1])
    ext, first, second, third, part = call(
        functools.partial(front_kernel, grid),
        "front",
        20,
        (
            shape(3, total_rows, 2, depth, LANES),
            shape(rows + 4, 2, depth, LANES),
            shape(rows + 2, 2, depth, LANES),
            shape(rows, 1, depth, LANES),
            shape(devices, LANES),
        ),
        (
            guarded_size((LINKS + 1) * (pairs + 8), depth),
            (rows + 4, 2, depth, LANES),
            padded_size(3 * (pairs + 12), depth),
            padded_size(3 * (pairs + 12), depth),
        ),
    )(own, mid, got_a, got_b, table)
    parts = lax.all_to_all(part, ("gx", "gy"), 0, 0, tiled=True)
    adjoint, sens = call(
        functools.partial(back_kernel, grid),
        "back",
        24,
        (shape(*block), shape(*block)),
        (
            guarded_size((LINKS + 1) * (pairs + 20), depth),
            (rows + 10, 2, depth, LANES),
            padded_size(3 * (2 * 10 + 2 * 10 + pairs + 16), depth),
            (rows + 6, 2, depth, LANES),
            padded_size(3 * pairs + 4 * (3 + 2 + 1), depth),
            (3, rows + 4, 2, depth, LANES),
            (2, rows + 4, 2, depth, LANES),
        ),
    )(ext, first, second, third, table, plate)
    return call(
        functools.partial(scale_kernel, float(depth * rows * width * devices)),
        "scale",
        2,
        (shape(*block), shape(*block)),
    )(parts, adjoint, sens)


def solution(mesh):
    block = P(None, "gx", "gy")
    return jax.shard_map(
        local,
        mesh=mesh,
        in_specs=(block, block, block, block, P(), P(), P()),
        out_specs=(block, block),
        check_vma=False,
    )
```

```python
import functools

import jax
import jax.numpy as jnp
from jax import lax
from jax.experimental import pallas as pl
from jax.experimental.pallas import tpu as pltpu
from jax.sharding import PartitionSpec as P

STEPS = 3
STEP_SCALE = 0.06
COOL_TEMP = 0.85
AGE_BETA = 8.0
HALF_OFFSETS = [
    (first, second, third)
    for first in (-1, 0, 1)
    for second in (-1, 0, 1)
    for third in (-1, 0, 1)
    if (first, second, third) > (0, 0, 0)
]
LINKS = len(HALF_OFFSETS)
HALO = 2 * STEPS
LANES = 128
SLOT = 16
T0, ID, COEFF = 0, 1, 2
SENT = (HALO, HALO - 1, HALO - 1)
PLACE = (3, 3 + HALO, 3 + 2 * HALO - 1)
PAYLOAD = 3 + sum(SENT)
PAD = 8
GUARD = 8
PARTS = 7


def lane_of(shape):
    return lax.broadcasted_iota(jnp.int32, shape, len(shape) - 1)


def copy_in(pairs, sems):
    copies = [
        pltpu.make_async_copy(source, target, sems.at[i])
        for i, (source, target) in enumerate(pairs)
    ]
    for copy in copies:
        copy.start()
    for copy in copies:
        copy.wait()


def table_kernel(principal_in, angles_in, aging_in, table, principal, angles, aging, line, sems):
    copy_in(((principal_in, principal), (angles_in, angles), (aging_in, aging)), sems)
    count = aging.shape[1]
    line[...] = jnp.zeros_like(line)
    line[0:3, 0:count] = principal[...]
    line[3:6, 0:count] = angles[...]
    line[6:7, 0:count] = aging[...]
    raw = pltpu.roll(line[...], 1, 1)
    p = [raw[k : k + 1] for k in range(3)]
    cosine, sine = jnp.cos(raw[3:6]), jnp.sin(raw[3:6])
    c1, c2, c3 = cosine[0:1], cosine[1:2], cosine[2:3]
    s1, s2, s3 = sine[0:1], sine[1:2], sine[2:3]
    columns = [
        (c1 * c3 - s1 * c2 * s3, s1 * c3 + c1 * c2 * s3, s2 * s3),
        (-c1 * s3 - s1 * c2 * c3, -s1 * s3 + c1 * c2 * c3, s2 * c3),
        (s1 * s2, -c1 * s2, c2),
    ]
    rows = []
    for i, j, factor in ((0, 0, 1), (1, 1, 1), (2, 2, 1), (0, 1, 2), (0, 2, 2), (1, 2, 2)):
        total = sum(p[k] * (columns[k][i] * columns[k][j]) for k in range(3))
        rows.append(STEP_SCALE * factor * total)
    rows.append(raw[6:7])
    for k, row in enumerate(rows):
        table[k] = jnp.broadcast_to(row, (8, LANES))


def pack_kernel(temp_in, material_in, plate_in, cooling_in, own, pack, temp, material, plate, cooling, sems):
    copy_in(
        ((temp_in, temp), (material_in, material), (plate_in, plate), (cooling_in, cooling)), sems
    )
    depth, rows, _ = temp.shape
    lane = lane_of((depth, LANES))
    packs = [jnp.zeros((depth, LANES), jnp.float32) for _ in range(3)]
    for x in range(rows):
        fields = (
            temp[:, x, :],
            (material[:, x, :] + 1).astype(jnp.float32),
            cooling[:, x, :] * plate[:, x, :].astype(jnp.float32),
        )
        mine = (lane >= SLOT * x) & (lane < SLOT * (x + 1))
        for f in range(3):
            own[f, x] = fields[f]
            moved = pltpu.roll(fields[f], (SLOT * x + HALO) % LANES, 1)
            packs[f] = jnp.where(mine, moved, packs[f])
    for f in range(3):
        pack[f] = packs[f]


def middle_kernel(last_y, own, side_a, side_b, mid, send_a, send_b):
    _, rows, depth, _ = own.shape
    at_y = lax.axis_index("gy")
    even_y = lax.rem(at_y, 2) == 0
    even_x = lax.rem(lax.axis_index("gx"), 2) == 0
    from_left = lax.rem(lane_of((depth, LANES)), SLOT) < HALO
    for f in range(3):
        left = jnp.where(at_y == 0, 0.0, jnp.where(even_y, side_b[f], side_a[f]))
        right = jnp.where(at_y == last_y, 0.0, jnp.where(even_y, side_a[f], side_b[f]))
        value = jnp.where(from_left, left, right)
        mid[f] = value
        send_a[f] = value
        send_b[f] = value
    for f in range(3):
        count = SENT[f]
        first_a = jnp.where(even_x, rows - count, 0)
        first_b = jnp.where(even_x, 0, rows - count)
        for r in range(count):
            send_a[PLACE[f] + r] = own[f, first_a + r]
            send_b[PLACE[f] + r] = own[f, first_b + r]


class Rows:
    def __init__(self):
        self.where = {}

    def flat(self, ref, rows, depth, pad, first_block=0, tiles=(0, 1)):
        block = first_block
        for r in rows:
            for t in tiles:
                start = block * (pad + depth) + (pad or GUARD)
                self.where[r, t] = (ref, None, start)
                block += 1
        return block

    def stacked(self, ref, rows, lead=(), first=0, tiles=(0, 1)):
        for r in rows:
            for t in tiles:
                self.where[r, t] = (ref, (*lead, r - first, t), 0)

    def of(self, r, t, size, offset=0):
        ref, index, start = self.where[r, t]
        if index is None:
            return ref[pl.ds(start + offset, size)]
        return ref[(*index, pl.ds(offset, size))]

    def put(self, r, t, value, offset=0):
        ref, index, start = self.where[r, t]
        if index is None:
            ref[pl.ds(start + offset, value.shape[0])] = value
        else:
            ref[(*index, pl.ds(offset, value.shape[0]))] = value


def clear_pads(ref, blocks, depth):
    zero = jnp.zeros((PAD, LANES), jnp.float32)
    for block in range(blocks + 1):
        ref[pl.ds(block * (PAD + depth), PAD)] = zero


def lane_shift(pair, by):
    lane = lane_of(pair[0].shape)
    moved = [pltpu.roll(value, (-by) % LANES, 1) for value in pair]
    edge = lane == (LANES - 1 if by > 0 else 0)
    return [jnp.where(edge, moved[1 - t], moved[t]) for t in (0, 1)]


def put_shifted(fields, r, pair):
    for by in (-1, 0, 1):
        moved = pair if by == 0 else lane_shift(pair, by)
        for t in (0, 1):
            fields[by].put(r, t, moved[t])


def advance(weights, keep, coeff, fields, rows, tiles, depth, done):
    for t in tiles:
        for half in range(depth // 8):
            base = 8 * half
            window = {}
            for r in rows:
                for other in (r - 1, r, r + 1):
                    if other not in window:
                        window[other] = {
                            (oz, oy): fields[oy].of(other, t, 8, base + oz)
                            for oz in (-1, 0, 1)
                            for oy in (-1, 0, 1)
                        }
                total = coeff.of(r, t, 8, base) * COOL_TEMP
                total = total + keep.of(r, t, 8, base) * window[r][0, 0]
                for k, (oz, ox, oy) in enumerate(HALF_OFFSETS):
                    both = window[r + ox][oz, oy] + window[r - ox][-oz, -oy]
                    total = total + weights[k].of(r, t, 8, base) * both
                done(r, t, base, total)
                window.pop(r - 1)


def reach(at, size):
    above = jnp.where(at < size - 1, 1.0, 0.0)
    below = jnp.where(at > 0, 1.0, 0.0)
    return above + below, above - below


def expand(table, weights, keep, ids, coeff, rows, grid, own_rows, depth):
    tables = [table[k] for k in range(PARTS)]
    quarter, ninth = 0.25, 1.0 / 9.0
    lane = lane_of((8, LANES))
    first_y = lax.axis_index("gy") * LANES
    first_x = lax.axis_index("gx") * own_rows - HALO
    for t in (0, 1):
        y = first_y + (lane if t == 0 else jnp.where(lane < LANES // 2, lane + LANES, lane - LANES))
        sum_y, dif_y = reach(y, grid[1])
        for half in range(depth // 8):
            z = lax.broadcasted_iota(jnp.int32, (8, LANES), 0) + 8 * half
            sum_z, dif_z = reach(z, depth)
            zz_0, zz_1 = sum_z * (1.0 + quarter * sum_y), sum_z * (quarter + ninth * sum_y)
            yy_0, yy_1 = sum_y * (1.0 + quarter * sum_z), sum_y * (quarter + ninth * sum_z)
            xx_1 = 1.0 + quarter * (sum_z + sum_y) + ninth * sum_z * sum_y
            zx_1 = dif_z * (quarter + ninth * sum_y)
            xy_1 = dif_y * (quarter + ninth * sum_z)
            zy_0, zy_1 = quarter * dif_z * dif_y, ninth * dif_z * dif_y
            for r in rows:
                sum_x, dif_x = reach(first_x + r, grid[0])
                part = ids.of(r, t, 8, 8 * half).astype(jnp.int32)
                zz, xx, yy, zx, zy, xy, aging = (
                    jnp.take_along_axis(entry, part, axis=1, mode="promise_in_bounds")
                    for entry in tables
                )
                near = (
                    zz * (zz_0 + sum_x * zz_1)
                    + yy * (yy_0 + sum_x * yy_1)
                    + zy * (zy_0 + sum_x * zy_1)
                    + xx * (sum_x * xx_1)
                    + dif_x * (zx * zx_1 + xy * xy_1)
                )
                keep.put(r, t, 1.0 - (coeff.of(r, t, 8, 8 * half) + near), 8 * half)
                found = {(1, 0, 0): zz, (0, 1, 0): xx, (0, 0, 1): yy}
                for first, second, cross, one, two in (
                    (zz, xx, zx, (1, 1, 0), (1, -1, 0)),
                    (zz, yy, zy, (1, 0, 1), (1, 0, -1)),
                    (xx, yy, xy, (0, 1, 1), (0, 1, -1)),
                ):
                    mean = (first + second) * quarter
                    cross = cross * quarter
                    found[one], found[two] = mean + cross, mean - cross
                trace = (zz + xx + yy) * ninth
                zx, zy, xy = zx * ninth, zy * ninth, xy * ninth
                up, down = trace + zx, trace - zx
                plus, minus = zy + xy, zy - xy
                found[1, 1, 1], found[1, 1, -1] = up + plus, up - plus
                found[1, -1, 1], found[1, -1, -1] = down + minus, down - minus
                for k, offset in enumerate(HALF_OFFSETS):
                    weights[k].put(r, t, found[offset], 8 * half)
                weights[LINKS].put(r, t, aging, 8 * half)


def rate_of(state):
    good = state > 0.5
    inverse = 1.0 / jnp.where(good, state, 1.0)
    return jnp.where(good, jnp.exp(AGE_BETA * (1.0 - inverse)), 0.0), inverse


class Plan:
    def __init__(self, rows):
        self.rows = rows
        self.middle = HALO + rows // 2

    def cone(self, radius):
        return range(HALO - radius, HALO + self.rows + radius)

    def ring(self, radius, inner):
        middle = self.cone(inner)
        return [r for r in self.cone(radius) if r not in middle]


def weight_rows(weights, ref, rows, depth):
    block = 0
    for field in weights:
        block = field.flat(ref, rows, depth, 0, block)


def shifted_rows(fields, ref, rows, depth, block=0):
    for oy in (-1, 0, 1):
        block = fields[oy].flat(ref, rows, depth, PAD, block)
    return block


def new_weights():
    return [Rows() for _ in range(LINKS + 1)]


def new_shifted():
    return {oy: Rows() for oy in (-1, 0, 1)}


def halves(rows, middle):
    return [r for r in rows if r < middle], [r for r in rows if r >= middle]


def march(n, weights, keep, coeff, source, target, out, rows, tiles, depth, loss):
    def done(r, t, base, value):
        out.put(r, t, value, base)
        if loss is not None and t == 0 and loss[0] <= r < loss[1]:
            rate, _ = rate_of(value)
            loss[2].append(weights[LINKS].of(r, 0, 8, base) * rate)

    for part in rows if isinstance(rows, tuple) else (rows,):
        advance(weights, keep, coeff, source, part, tiles, depth, done)
        if target is not None:
            for r in part:
                put_shifted(target, r, [out.of(r, t, depth) for t in (0, 1)])


def padded_size(blocks, depth):
    return (blocks * (PAD + depth) + PAD, LANES)


def guarded_size(blocks, depth):
    return (blocks * depth + 2 * GUARD, LANES)


def total_of(terms):
    total = terms[0]
    for term in terms[1:]:
        total = total + term
    return total


def unpack(target, f, at, source, x, halo_lane):
    moved = pltpu.roll(source, (-(SLOT * x + HALO)) % LANES, 1)
    target[(f, *at)] = jnp.where(halo_lane, moved, 0.0)


def core_kernel(
    grid, own, mid, table,
    halo, weights_ref, keep_ref, start_ref, first, first_ref, second, second_ref, third, loss_ref,
):
    _, rows, depth, _ = own.shape
    plan = Plan(rows)
    lane = lane_of((depth, LANES))
    halo_lane = (lane < HALO) | (lane >= LANES - HALO)
    for f in range(3):
        for x in range(rows):
            unpack(halo, f, (x,), mid[f], x, halo_lane)
    temp, ids, coeff = own_fields(own, halo, plan)
    weights, keep = new_weights(), Rows()
    weight_rows(weights, weights_ref, plan.cone(0), depth)
    keep.stacked(keep_ref, plan.cone(0), (), HALO)
    shifted, outs = [new_shifted() for _ in range(3)], [Rows() for _ in range(3)]
    for n, (ref, out) in enumerate(((start_ref, first), (first_ref, second), (second_ref, third))):
        clear_pads(ref, shifted_rows(shifted[n], ref, plan.cone(-n), depth), depth)
        outs[n].stacked(out, plan.cone(-n - 1), (), HALO + n + 1)
    expand(table, weights, keep, ids, coeff, plan.cone(0), grid, rows, depth)
    for r in plan.cone(0):
        put_shifted(shifted[0], r, [temp.of(r, t, depth) for t in (0, 1)])
    loss = (HALO, HALO + rows, [])
    for n in range(STEPS):
        target = shifted[n + 1] if n < 2 else None
        tiles = (0, 1) if n < 2 else (0,)
        march(n, weights, keep, coeff, shifted[n], target, outs[n], plan.cone(-n - 1), tiles, depth, loss)
    loss_ref[...] = total_of(loss[2])


def own_fields(own, halo, plan):
    fields = (Rows(), Rows(), Rows())
    for f, field in enumerate(fields):
        for r in plan.cone(0):
            field.where[r, 0] = (own, (f, r - HALO), 0)
            field.where[r, 1] = (halo, (f, r - HALO), 0)
    return fields


def all_fields(own, halo, ext, plan):
    fields = own_fields(own, halo, plan)
    for f, field in enumerate(fields):
        for i, r in enumerate(plan.ring(HALO, 0)):
            for t in (0, 1):
                field.where[r, t] = (ext, (f, i, t), 0)
    return fields


def front_kernel(
    grid, own, halo, got_a, got_b, table, weights_in, keep_in, start_in, first_in, second_in, loss_in,
    ext, first, second, third, part,
    weights_ref, keep_ref, start_ref, first_ref, second_ref,
):
    _, rows, depth, _ = own.shape
    plan = Plan(rows)
    even = lax.rem(lax.axis_index("gx"), 2) == 0
    lane = lane_of((depth, LANES))
    halo_lane = (lane < HALO) | (lane >= LANES - HALO)
    for f in range(3):
        base_a = jnp.where(even, HALO, HALO - SENT[f])
        base_b = jnp.where(even, HALO - SENT[f], HALO)
        for r in range(SENT[f]):
            ext[f, base_a + r, 0] = got_a[PLACE[f] + r]
            ext[f, base_b + r, 0] = got_b[PLACE[f] + r]
        low = jnp.where(even, got_b[f], got_a[f])
        high = jnp.where(even, got_a[f], got_b[f])
        for r in range(HALO):
            unpack(ext, f, (r, 1), low, rows - HALO + r, halo_lane)
            unpack(ext, f, (HALO + r, 1), high, r, halo_lane)

    temp, ids, coeff = all_fields(own, halo, ext, plan)
    weights, keep = new_weights(), Rows()
    outer = plan.ring(2, 0)
    weight_rows(weights, weights_in, plan.cone(0), depth)
    weight_rows(weights, weights_ref, outer, depth)
    keep.stacked(keep_in, plan.cone(0), (), HALO)
    for i, r in enumerate(outer):
        for t in (0, 1):
            keep.where[r, t] = (keep_ref, (i, t), 0)
    shifted, outs = [new_shifted() for _ in range(3)], [Rows() for _ in range(3)]
    for n, (given, ref, out) in enumerate(
        ((start_in, start_ref, first), (first_in, first_ref, second), (second_in, second_ref, third))
    ):
        shifted_rows(shifted[n], given, plan.cone(-n), depth)
        fresh = plan.ring(3 - n, -n)
        clear_pads(ref, shifted_rows(shifted[n], ref, fresh, depth), depth)
        for i, r in enumerate(plan.ring(2 - n, -n - 1)):
            for t in (0, 1) if n < 2 else (0,):
                outs[n].where[r, t] = (out, (i, t), 0)
    expand(table, weights, keep, ids, coeff, outer, grid, rows, depth)
    for r in plan.ring(3, 0):
        put_shifted(shifted[0], r, [temp.of(r, t, depth) for t in (0, 1)])
    loss = (HALO, HALO + rows, [])
    for n in range(STEPS):
        ring = halves(plan.ring(2 - n, -n - 1), plan.middle)
        target = shifted[n + 1] if n < 2 else None
        tiles = (0, 1) if n < 2 else (0,)
        march(n, weights, keep, coeff, shifted[n], target, outs[n], ring, tiles, depth, loss)
    total = loss_in[...] + total_of(loss[2])
    part[...] = jnp.broadcast_to(jnp.sum(total, axis=0, keepdims=True), part.shape)


def back_kernel(
    grid, own, halo, ext, first_core, second_core, third_core, first_in, second_in, third_in, table, plate,
    adjoint_out, sens_out,
    weights_ref, keep_ref, states_ref, third_ref, adjoint_ref, sums_ref, drive_ref,
):
    _, rows, depth, _ = own.shape
    plan = Plan(rows)
    temp, ids, coeff = all_fields(own, halo, ext, plan)
    for start in (0, weights_ref.shape[0] - GUARD):
        weights_ref[pl.ds(start, GUARD)] = jnp.zeros((GUARD, LANES), jnp.float32)
    weights, keep = new_weights(), Rows()
    weight_rows(weights, weights_ref, plan.cone(5), depth)
    keep.stacked(keep_ref, plan.cone(5), (), HALO - 5)
    shifted, block = [new_shifted() for _ in range(3)], 0
    for n in range(3):
        held = plan.ring(6 - n, 1 - n) if n < 2 else plan.cone(4)
        block = shifted_rows(shifted[n], states_ref, held, depth, block)
    clear_pads(states_ref, block, depth)
    states = [temp, Rows(), Rows(), Rows()]
    for n, (core, given) in enumerate(
        ((first_core, first_in), (second_core, second_in), (third_core, third_in))
    ):
        tiles = (0, 1) if n < 2 else (0,)
        states[n + 1].stacked(core, plan.cone(-n - 1), (), HALO + n + 1, tiles)
        for i, r in enumerate(plan.ring(2 - n, -n - 1)):
            for t in tiles:
                states[n + 1].where[r, t] = (given, (i, t), 0)

    expand(table, weights, keep, ids, coeff, plan.cone(5), grid, rows, depth)
    for r in plan.ring(6, 1):
        put_shifted(shifted[0], r, [temp.of(r, t, depth) for t in (0, 1)])
    for r in plan.ring(2, 0):
        put_shifted(shifted[1], r, [states[1].of(r, t, depth) for t in (0, 1)])
    for r in plan.cone(1):
        put_shifted(shifted[2], r, [states[2].of(r, t, depth) for t in (0, 1)])
    states[2] = shifted[2][0]
    found = Rows()
    found.stacked(third_ref, plan.cone(3), (), HALO - 3)
    for key, place in found.where.items():
        states[3].where.setdefault(key, place)
    for n in range(STEPS):
        fresh = plan.ring(5 - n, 2 - n)
        out = states[3] if n == 2 else shifted[n + 1][0]

        def done(r, t, base, value):
            out.put(r, t, value, base)

        for part in halves(fresh, plan.middle):
            advance(weights, keep, coeff, shifted[n], part, (0, 1), depth, done)
        if n == 2:
            advance(weights, keep, coeff, shifted[n], plan.cone(0), (1,), depth, done)
            continue
        for r in fresh:
            pair = [out.of(r, t, depth) for t in (0, 1)]
            for by in (-1, 1):
                moved = lane_shift(pair, by)
                for t in (0, 1):
                    shifted[n + 1][by].put(r, t, moved[t])

    vectors, block = [], 0
    for n in range(3):
        vectors.append(Rows())
        block = vectors[n].flat(adjoint_ref, plan.cone(3 - n), depth, PAD, block)
    clear_pads(adjoint_ref, block, depth)
    drives = [None, Rows(), Rows(), vectors[0]]
    drives[1].stacked(drive_ref, plan.cone(1), (0,), HALO - 2)
    drives[2].stacked(drive_ref, plan.cone(2), (1,), HALO - 2)
    for n in range(1, 4):
        for r in plan.cone(n):
            for t in (0, 1):
                rate, inverse = rate_of(states[n].of(r, t, depth))
                factor = weights[LINKS].of(r, t, depth) * AGE_BETA
                drives[n].put(r, t, factor * rate * (inverse * inverse))
    sums = {}
    for oy in (-1, 0, 1):
        sums[oy] = Rows()
        sums[oy].stacked(sums_ref, plan.cone(2), (oy + 1,), HALO - 2)
    for n in range(3):
        vector = vectors[n]
        targets = plan.cone(2 - n)
        for t in (0, 1):
            for half in range(depth // 8):
                base = 8 * half
                totals = {}
                for source in plan.cone(3 - n):
                    reads = {oz: vector.of(source, t, 8, base - oz) for oz in (-1, 0, 1)}
                    for k, offset in enumerate(HALF_OFFSETS):
                        product = {}
                        for sign in (1, -1):
                            oz, ox, oy = (sign * o for o in offset)
                            if oz not in product:
                                weight = weights[k].of(source, t, 8, base - oz)
                                product[oz] = reads[oz] * weight
                            key = (source + ox, oy)
                            if key[0] in targets:
                                totals[key] = (
                                    totals[key] + product[oz] if key in totals else product[oz]
                                )
                    if source - 1 in targets:
                        for oy in (-1, 0, 1):
                            sums[oy].put(source - 1, t, totals.pop((source - 1, oy)), base)
        for r in targets:
            plus = lane_shift([sums[1].of(r, t, depth) for t in (0, 1)], -1)
            minus = lane_shift([sums[-1].of(r, t, depth) for t in (0, 1)], 1)
            for t in (0, 1) if n < 2 else (0,):
                result = (
                    keep.of(r, t, depth) * vector.of(r, t, depth)
                    + sums[0].of(r, t, depth)
                    + (plus[t] + minus[t])
                )
                if n < 2:
                    vectors[n + 1].put(r, t, result + drives[2 - n].of(r, t, depth))
                else:
                    adjoint_out[:, r - HALO, :] = result
    for r in plan.cone(0):
        total = None
        for n in range(3):
            term = vectors[2 - n].of(r, 0, depth) * (states[n].of(r, 0, depth) - COOL_TEMP)
            total = term if total is None else total + term
        sens_out[:, r - HALO, :] = -total * plate[:, r - HALO, :].astype(jnp.float32)


def scale_kernel(cells, parts, adjoint, sens, adjoint_out, sens_out):
    row = jnp.sum(parts[...], axis=0, keepdims=True)
    scale = cells / jnp.sum(row, axis=1, keepdims=True)
    adjoint_out[...] = adjoint[...] * scale.reshape(1, 1, 1)
    sens_out[...] = sens[...] * scale.reshape(1, 1, 1)


def pairing(count, first, ring):
    out = {}
    for i in range(first, count - 1, 2):
        out[i], out[i + 1] = i + 1, i
    if ring and 0 not in out:
        out[0], out[count - 1] = count - 1, 0
    return out


def swap(value, sizes, axis, first, ring=False):
    count_x, count_y = sizes
    partner = pairing(sizes[axis], first, ring)
    pairs = []
    for i in range(count_x):
        for j in range(count_y):
            other = partner.get((i, j)[axis])
            if other is not None:
                target = (other, j) if axis == 0 else (i, other)
                pairs.append((i * count_y + j, target[0] * count_y + target[1]))
    return lax.ppermute(value, ("gx", "gy"), pairs)


def local(initial_temp, material, plate, cooling, principal, angles, aging_scale):
    depth, rows, width = initial_temp.shape
    sizes = (lax.axis_size("gx"), lax.axis_size("gy"))
    devices = sizes[0] * sizes[1]
    f32 = jnp.float32

    def shape(*dims):
        return jax.ShapeDtypeStruct(dims, f32)

    def call(kernel, name, mib, out_shape, scratch=(), **specs):
        return pl.pallas_call(
            kernel,
            out_shape=out_shape,
            scratch_shapes=[
                pltpu.VMEM(dims, f32) if isinstance(dims, tuple) else dims for dims in scratch
            ],
            name=name,
            compiler_params=pltpu.CompilerParams(vmem_limit_bytes=mib * 2**20),
            **specs,
        )

    block = (depth, rows, LANES)
    own, pack = call(
        pack_kernel,
        "pack",
        2,
        (shape(3, rows, depth, LANES), shape(3, depth, LANES)),
        (
            block,
            pltpu.VMEM(block, jnp.int32),
            pltpu.VMEM(block, jnp.int32),
            block,
            pltpu.SemaphoreType.DMA((4,)),
        ),
        in_specs=[pl.BlockSpec(memory_space=pltpu.HBM)] * 4,
    )(*(pltpu.with_memory_space_constraint(x, pltpu.HBM) for x in (initial_temp, material, plate, cooling)))
    side_b = swap(pack, sizes, 1, 1, True)
    side_a = swap(pack, sizes, 1, 0)
    mid, send_a, send_b = call(
        functools.partial(middle_kernel, sizes[1] - 1),
        "middle",
        2,
        (shape(3, depth, LANES), shape(PAYLOAD, depth, LANES), shape(PAYLOAD, depth, LANES)),
    )(own, side_a, side_b)
    got_b = swap(send_b, sizes, 0, 1)
    got_a = swap(send_a, sizes, 0, 0)
    small = [principal.T, angles.T, aging_scale[None]]
    table = call(
        table_kernel,
        "table",
        2,
        shape(PARTS, 8, LANES),
        (*(x.shape for x in small), (8, LANES), pltpu.SemaphoreType.DMA((3,))),
        in_specs=[pl.BlockSpec(memory_space=pltpu.HBM)] * 3,
    )(*(pltpu.with_memory_space_constraint(x, pltpu.HBM) for x in small))

    pairs = 2 * rows
    grid = (rows * sizes[0], width * sizes[1])
    halo, weights, keep, start, first_core, first_moved, second_core, second_moved, third_core, loss = call(
        functools.partial(core_kernel, grid),
        "core",
        8,
        (
            shape(3, rows, depth, LANES),
            shape(*guarded_size((LINKS + 1) * pairs, depth)),
            shape(rows, 2, depth, LANES),
            shape(*padded_size(3 * pairs, depth)),
            shape(rows - 2, 2, depth, LANES),
            shape(*padded_size(3 * (pairs - 4), depth)),
            shape(rows - 4, 2, depth, LANES),
            shape(*padded_size(3 * (pairs - 8), depth)),
            shape(rows - 6, 1, depth, LANES),
            shape(8, LANES),
        ),
    )(own, mid, table)
    ext, first, second, third, part = call(
        functools.partial(front_kernel, grid),
        "front",
        16,
        (
            shape(3, 2 * HALO, 2, depth, LANES),
            shape(6, 2, depth, LANES),
            shape(6, 2, depth, LANES),
            shape(6, 1, depth, LANES),
            shape(devices, LANES),
        ),
        (
            guarded_size((LINKS + 1) * 8, depth),
            (4, 2, depth, LANES),
            padded_size(3 * 12, depth),
            padded_size(3 * 12, depth),
            padded_size(3 * 12, depth),
        ),
    )(own, halo, got_a, got_b, table, weights, keep, start, first_moved, second_moved, loss)
    parts = lax.all_to_all(part, ("gx", "gy"), 0, 0, tiled=True)
    adjoint, sens = call(
        functools.partial(back_kernel, grid),
        "back",
        24,
        (shape(*block), shape(*block)),
        (
            guarded_size((LINKS + 1) * (pairs + 20), depth),
            (rows + 10, 2, depth, LANES),
            padded_size(3 * (2 * 10 + 2 * 10 + pairs + 16), depth),
            (rows + 6, 2, depth, LANES),
            padded_size(3 * pairs + 4 * (3 + 2 + 1), depth),
            (3, rows + 4, 2, depth, LANES),
            (2, rows + 4, 2, depth, LANES),
        ),
    )(own, halo, ext, first_core, second_core, third_core, first, second, third, table, plate)
    return call(
        functools.partial(scale_kernel, float(depth * rows * width * devices)),
        "scale",
        2,
        (shape(*block), shape(*block)),
    )(parts, adjoint, sens)


def solution(mesh):
    block = P(None, "gx", "gy")
    return jax.shard_map(
        local,
        mesh=mesh,
        in_specs=(block, block, block, block, P(), P(), P()),
        out_specs=(block, block),
        check_vma=False,
    )
```

```python
import functools

import jax
import jax.numpy as jnp
from jax import lax
from jax.experimental import pallas as pl
from jax.experimental.pallas import tpu as pltpu
from jax.sharding import PartitionSpec as P


STEPS = 3
STEP_SCALE = 0.06
COOL_TEMP = 0.85
AGE_BETA = 8.0
HALF_OFFSETS = [
    (first, second, third)
    for first in (-1, 0, 1)
    for second in (-1, 0, 1)
    for third in (-1, 0, 1)
    if (first, second, third) > (0, 0, 0)
]
LINKS = len(HALF_OFFSETS)
HALO = 2 * STEPS
LANES = 128
SLOT = 16
SENT = (HALO, HALO - 1, HALO - 1)
PLACE = (3, 3 + HALO, 3 + 2 * HALO - 1)
PAYLOAD = 3 + sum(SENT)
PAD = 8
GUARD = 8
PARTS = 7


def lane_of(shape):
    return lax.broadcasted_iota(jnp.int32, shape, len(shape) - 1)


def put_table(principal, angles, aging, table, line):
    count = aging.shape[1]
    line[...] = jnp.zeros_like(line)
    line[0:3, 0:count] = principal[...]
    line[3:6, 0:count] = angles[...]
    line[6:7, 0:count] = aging[...]
    raw = pltpu.roll(line[...], 1, 1)
    p = [raw[k : k + 1] for k in range(3)]
    cosine, sine = jnp.cos(raw[3:6]), jnp.sin(raw[3:6])
    c1, c2, c3 = cosine[0:1], cosine[1:2], cosine[2:3]
    s1, s2, s3 = sine[0:1], sine[1:2], sine[2:3]
    columns = [
        (c1 * c3 - s1 * c2 * s3, s1 * c3 + c1 * c2 * s3, s2 * s3),
        (-c1 * s3 - s1 * c2 * c3, -s1 * s3 + c1 * c2 * c3, s2 * c3),
        (s1 * s2, -c1 * s2, c2),
    ]
    rows = []
    for i, j, factor in ((0, 0, 1), (1, 1, 1), (2, 2, 1), (0, 1, 2), (0, 2, 2), (1, 2, 2)):
        total = sum(p[k] * (columns[k][i] * columns[k][j]) for k in range(3))
        rows.append(STEP_SCALE * factor * total)
    rows.append(raw[6:7])
    for k, row in enumerate(rows):
        table[k] = jnp.broadcast_to(row, (8, LANES))


def pack_kernel(
    principal_in, angles_in, aging_in, temp_in, material_in, plate_in, cooling_in,
    own, pack, send_b, table,
    principal, angles, aging, temp, material, plate, cooling, line, sems,
):
    pairs = (
        (principal_in, principal), (angles_in, angles), (aging_in, aging),
        (temp_in, temp), (material_in, material), (plate_in, plate), (cooling_in, cooling),
    )
    copies = [
        pltpu.make_async_copy(source, target, sems.at[i])
        for i, (source, target) in enumerate(pairs)
    ]
    for copy in copies:
        copy.start()
    for copy in copies[:3]:
        copy.wait()
    put_table(principal, angles, aging, table, line)
    for copy in copies[3:]:
        copy.wait()
    depth, rows, _ = temp.shape
    lane = lane_of((depth, LANES))
    packs = [jnp.zeros((depth, LANES), jnp.float32) for _ in range(3)]
    for x in range(rows):
        fields = (
            temp[:, x, :],
            (material[:, x, :] + 1).astype(jnp.float32),
            cooling[:, x, :] * plate[:, x, :].astype(jnp.float32),
        )
        mine = (lane >= SLOT * x) & (lane < SLOT * (x + 1))
        for f in range(3):
            own[f, x] = fields[f]
            moved = pltpu.roll(fields[f], (SLOT * x + HALO) % LANES, 1)
            packs[f] = jnp.where(mine, moved, packs[f])
    even_x = lax.rem(lax.axis_index("gx"), 2) == 0
    for f in range(3):
        pack[f] = packs[f]
        count = SENT[f]
        first_b = jnp.where(even_x, 0, rows - count)
        for r in range(count):
            send_b[PLACE[f] - 3 + r] = own[f, first_b + r]


def middle_kernel(last_y, own, side_a, side_b, mid, send_a):
    _, rows, depth, _ = own.shape
    at_y = lax.axis_index("gy")
    even_y = lax.rem(at_y, 2) == 0
    even_x = lax.rem(lax.axis_index("gx"), 2) == 0
    from_left = lax.rem(lane_of((depth, LANES)), SLOT) < HALO
    for f in range(3):
        left = jnp.where(at_y == 0, 0.0, jnp.where(even_y, side_b[f], side_a[f]))
        right = jnp.where(at_y == last_y, 0.0, jnp.where(even_y, side_a[f], side_b[f]))
        value = jnp.where(from_left, left, right)
        mid[f] = value
        send_a[f] = value
    for f in range(3):
        count = SENT[f]
        first_a = jnp.where(even_x, rows - count, 0)
        for r in range(count):
            send_a[PLACE[f] + r] = own[f, first_a + r]


class Rows:
    def __init__(self):
        self.where = {}

    def flat(self, ref, rows, depth, pad, first_block=0, tiles=(0, 1)):
        block = first_block
        for r in rows:
            for t in tiles:
                start = block * (pad + depth) + (pad or GUARD)
                self.where[r, t] = (ref, None, start)
                block += 1
        return block

    def stacked(self, ref, rows, lead=(), first=0, tiles=(0, 1)):
        for r in rows:
            for t in tiles:
                self.where[r, t] = (ref, (*lead, r - first, t), 0)

    def of(self, r, t, size, offset=0):
        ref, index, start = self.where[r, t]
        if index is None:
            return ref[pl.ds(start + offset, size)]
        return ref[(*index, pl.ds(offset, size))]

    def put(self, r, t, value, offset=0):
        ref, index, start = self.where[r, t]
        if index is None:
            ref[pl.ds(start + offset, value.shape[0])] = value
        else:
            ref[(*index, pl.ds(offset, value.shape[0]))] = value


def clear_pads(ref, blocks, depth):
    zero = jnp.zeros((PAD, LANES), jnp.float32)
    for block in range(blocks + 1):
        ref[pl.ds(block * (PAD + depth), PAD)] = zero


def lane_shift(pair, by):
    lane = lane_of(pair[0].shape)
    moved = [pltpu.roll(value, (-by) % LANES, 1) for value in pair]
    edge = lane == (LANES - 1 if by > 0 else 0)
    return [jnp.where(edge, moved[1 - t], moved[t]) for t in (0, 1)]


def put_shifted(fields, r, pair):
    for by in (-1, 0, 1):
        moved = pair if by == 0 else lane_shift(pair, by)
        for t in (0, 1):
            fields[by].put(r, t, moved[t])


def advance(weights, keep, coeff, fields, rows, tiles, depth, done):
    for t in tiles:
        for half in range(depth // 8):
            base = 8 * half
            window = {}
            for r in rows:
                for other in (r - 1, r, r + 1):
                    if other not in window:
                        window[other] = {
                            (oz, oy): fields[oy].of(other, t, 8, base + oz)
                            for oz in (-1, 0, 1)
                            for oy in (-1, 0, 1)
                        }
                total = coeff.of(r, t, 8, base) * COOL_TEMP
                total = total + keep.of(r, t, 8, base) * window[r][0, 0]
                for k, (oz, ox, oy) in enumerate(HALF_OFFSETS):
                    both = window[r + ox][oz, oy] + window[r - ox][-oz, -oy]
                    total = total + weights[k].of(r, t, 8, base) * both
                done(r, t, base, total)
                window.pop(r - 1)


def reach(at, size):
    above = jnp.where(at < size - 1, 1.0, 0.0)
    below = jnp.where(at > 0, 1.0, 0.0)
    return above + below, above - below


def expand(table, weights, keep, ids, coeff, rows, grid, own_rows, depth):
    tables = [table[k] for k in range(PARTS)]
    quarter, ninth = 0.25, 1.0 / 9.0
    lane = lane_of((8, LANES))
    first_y = lax.axis_index("gy") * LANES
    first_x = lax.axis_index("gx") * own_rows - HALO
    for t in (0, 1):
        y = first_y + (lane if t == 0 else jnp.where(lane < LANES // 2, lane + LANES, lane - LANES))
        sum_y, dif_y = reach(y, grid[1])
        for half in range(depth // 8):
            z = lax.broadcasted_iota(jnp.int32, (8, LANES), 0) + 8 * half
            sum_z, dif_z = reach(z, depth)
            zz_0, zz_1 = sum_z * (1.0 + quarter * sum_y), sum_z * (quarter + ninth * sum_y)
            yy_0, yy_1 = sum_y * (1.0 + quarter * sum_z), sum_y * (quarter + ninth * sum_z)
            xx_1 = 1.0 + quarter * (sum_z + sum_y) + ninth * sum_z * sum_y
            zx_1 = dif_z * (quarter + ninth * sum_y)
            xy_1 = dif_y * (quarter + ninth * sum_z)
            zy_0, zy_1 = quarter * dif_z * dif_y, ninth * dif_z * dif_y
            for r in rows:
                sum_x, dif_x = reach(first_x + r, grid[0])
                part = ids.of(r, t, 8, 8 * half).astype(jnp.int32)
                zz, xx, yy, zx, zy, xy, aging = (
                    jnp.take_along_axis(entry, part, axis=1, mode="promise_in_bounds")
                    for entry in tables
                )
                near = (
                    zz * (zz_0 + sum_x * zz_1)
                    + yy * (yy_0 + sum_x * yy_1)
                    + zy * (zy_0 + sum_x * zy_1)
                    + xx * (sum_x * xx_1)
                    + dif_x * (zx * zx_1 + xy * xy_1)
                )
                keep.put(r, t, 1.0 - (coeff.of(r, t, 8, 8 * half) + near), 8 * half)
                found = {(1, 0, 0): zz, (0, 1, 0): xx, (0, 0, 1): yy}
                for first, second, cross, one, two in (
                    (zz, xx, zx, (1, 1, 0), (1, -1, 0)),
                    (zz, yy, zy, (1, 0, 1), (1, 0, -1)),
                    (xx, yy, xy, (0, 1, 1), (0, 1, -1)),
                ):
                    mean = (first + second) * quarter
                    cross = cross * quarter
                    found[one], found[two] = mean + cross, mean - cross
                trace = (zz + xx + yy) * ninth
                zx, zy, xy = zx * ninth, zy * ninth, xy * ninth
                up, down = trace + zx, trace - zx
                plus, minus = zy + xy, zy - xy
                found[1, 1, 1], found[1, 1, -1] = up + plus, up - plus
                found[1, -1, 1], found[1, -1, -1] = down + minus, down - minus
                for k, offset in enumerate(HALF_OFFSETS):
                    weights[k].put(r, t, found[offset], 8 * half)
                weights[LINKS].put(r, t, aging, 8 * half)


def rate_of(state):
    good = state > 0.5
    inverse = 1.0 / jnp.where(good, state, 1.0)
    return jnp.where(good, jnp.exp(AGE_BETA * (1.0 - inverse)), 0.0), inverse


class Plan:
    def __init__(self, rows):
        self.rows = rows
        self.middle = HALO + rows // 2

    def cone(self, radius):
        return range(HALO - radius, HALO + self.rows + radius)

    def ring(self, radius, inner):
        middle = self.cone(inner)
        return [r for r in self.cone(radius) if r not in middle]


def weight_rows(weights, ref, rows, depth):
    block = 0
    for field in weights:
        block = field.flat(ref, rows, depth, 0, block)


def shifted_rows(fields, ref, rows, depth, block=0):
    for oy in (-1, 0, 1):
        block = fields[oy].flat(ref, rows, depth, PAD, block)
    return block


def new_weights():
    return [Rows() for _ in range(LINKS + 1)]


def new_shifted():
    return {oy: Rows() for oy in (-1, 0, 1)}


def halves(rows, middle):
    return [r for r in rows if r < middle], [r for r in rows if r >= middle]


def march(weights, keep, coeff, source, target, out, rows, tiles, depth, loss):
    def done(r, t, base, value):
        out.put(r, t, value, base)
        if loss is not None and t == 0 and loss[0] <= r < loss[1]:
            rate, _ = rate_of(value)
            loss[2].append(weights[LINKS].of(r, 0, 8, base) * rate)

    for part in rows if isinstance(rows, tuple) else (rows,):
        advance(weights, keep, coeff, source, part, tiles, depth, done)
        if target is not None:
            for r in part:
                put_shifted(target, r, [out.of(r, t, depth) for t in (0, 1)])


def padded_size(blocks, depth):
    return (blocks * (PAD + depth) + PAD, LANES)


def guarded_size(blocks, depth):
    return (blocks * depth + 2 * GUARD, LANES)


def total_of(terms):
    total = terms[0]
    for term in terms[1:]:
        total = total + term
    return total


def unpack(target, f, at, source, x, halo_lane):
    moved = pltpu.roll(source, (-(SLOT * x + HALO)) % LANES, 1)
    target[(f, *at)] = jnp.where(halo_lane, moved, 0.0)


def core_kernel(
    grid, own, mid, table,
    halo, weights_ref, keep_ref, start_ref, first, first_ref, second, second_ref, third, loss_ref,
):
    _, rows, depth, _ = own.shape
    plan = Plan(rows)
    lane = lane_of((depth, LANES))
    halo_lane = (lane < HALO) | (lane >= LANES - HALO)
    for f in range(3):
        for x in range(rows):
            unpack(halo, f, (x,), mid[f], x, halo_lane)
    temp, ids, coeff = own_fields(own, halo, plan)
    weights, keep = new_weights(), Rows()
    weight_rows(weights, weights_ref, plan.cone(0), depth)
    keep.stacked(keep_ref, plan.cone(0), (), HALO)
    shifted, outs = [new_shifted() for _ in range(3)], [Rows() for _ in range(3)]
    for n, (ref, out) in enumerate(((start_ref, first), (first_ref, second), (second_ref, third))):
        clear_pads(ref, shifted_rows(shifted[n], ref, plan.cone(-n), depth), depth)
        outs[n].stacked(out, plan.cone(-n - 1), (), HALO + n + 1)
    expand(table, weights, keep, ids, coeff, plan.cone(0), grid, rows, depth)
    for r in plan.cone(0):
        put_shifted(shifted[0], r, [temp.of(r, t, depth) for t in (0, 1)])
    loss = (HALO, HALO + rows, [])
    for n in range(STEPS):
        target = shifted[n + 1] if n < 2 else None
        tiles = (0, 1) if n < 2 else (0,)
        march(weights, keep, coeff, shifted[n], target, outs[n], plan.cone(-n - 1), tiles, depth, loss)
    loss_ref[...] = total_of(loss[2])


def own_fields(own, halo, plan):
    fields = (Rows(), Rows(), Rows())
    for f, field in enumerate(fields):
        for r in plan.cone(0):
            field.where[r, 0] = (own, (f, r - HALO), 0)
            field.where[r, 1] = (halo, (f, r - HALO), 0)
    return fields


def all_fields(own, halo, ext, plan):
    fields = own_fields(own, halo, plan)
    for f, field in enumerate(fields):
        for i, r in enumerate(plan.ring(HALO, 0)):
            for t in (0, 1):
                field.where[r, t] = (ext, (f, i, t), 0)
    return fields


def front_kernel(
    grid, own, halo, got_b, far_b, got_a, table, weights_in, keep_in, start_in, first_in, second_in, loss_in,
    ext, first, second, third, part,
    weights_ref, keep_ref, start_ref, first_ref, second_ref,
):
    _, rows, depth, _ = own.shape
    plan = Plan(rows)
    even = lax.rem(lax.axis_index("gx"), 2) == 0
    lane = lane_of((depth, LANES))
    halo_lane = (lane < HALO) | (lane >= LANES - HALO)
    for f in range(3):
        base_a = jnp.where(even, HALO, HALO - SENT[f])
        base_b = jnp.where(even, HALO - SENT[f], HALO)
        for r in range(SENT[f]):
            ext[f, base_a + r, 0] = got_a[PLACE[f] + r]
            ext[f, base_b + r, 0] = far_b[PLACE[f] - 3 + r]
        low = jnp.where(even, got_b[f], got_a[f])
        high = jnp.where(even, got_a[f], got_b[f])
        for r in range(HALO):
            unpack(ext, f, (r, 1), low, rows - HALO + r, halo_lane)
            unpack(ext, f, (HALO + r, 1), high, r, halo_lane)

    temp, ids, coeff = all_fields(own, halo, ext, plan)
    weights, keep = new_weights(), Rows()
    outer = plan.ring(2, 0)
    weight_rows(weights, weights_in, plan.cone(0), depth)
    weight_rows(weights, weights_ref, outer, depth)
    keep.stacked(keep_in, plan.cone(0), (), HALO)
    for i, r in enumerate(outer):
        for t in (0, 1):
            keep.where[r, t] = (keep_ref, (i, t), 0)
    shifted, outs = [new_shifted() for _ in range(3)], [Rows() for _ in range(3)]
    for n, (given, ref, out) in enumerate(
        ((start_in, start_ref, first), (first_in, first_ref, second), (second_in, second_ref, third))
    ):
        shifted_rows(shifted[n], given, plan.cone(-n), depth)
        fresh = plan.ring(3 - n, -n)
        clear_pads(ref, shifted_rows(shifted[n], ref, fresh, depth), depth)
        for i, r in enumerate(plan.ring(2 - n, -n - 1)):
            for t in (0, 1) if n < 2 else (0,):
                outs[n].where[r, t] = (out, (i, t), 0)
    expand(table, weights, keep, ids, coeff, outer, grid, rows, depth)
    for r in plan.ring(3, 0):
        put_shifted(shifted[0], r, [temp.of(r, t, depth) for t in (0, 1)])
    loss = (HALO, HALO + rows, [])
    for n in range(STEPS):
        ring = halves(plan.ring(2 - n, -n - 1), plan.middle)
        target = shifted[n + 1] if n < 2 else None
        tiles = (0, 1) if n < 2 else (0,)
        march(weights, keep, coeff, shifted[n], target, outs[n], ring, tiles, depth, loss)
    total = loss_in[...] + total_of(loss[2])
    part[...] = jnp.broadcast_to(jnp.sum(total, axis=0, keepdims=True), part.shape)


def back_kernel(
    grid, own, halo, ext, first_core, second_core, third_core, first_in, second_in, third_in, table, plate,
    adjoint_out, sens_out,
    weights_ref, keep_ref, states_ref, third_ref, adjoint_ref, sums_ref, drive_ref,
):
    _, rows, depth, _ = own.shape
    plan = Plan(rows)
    temp, ids, coeff = all_fields(own, halo, ext, plan)
    for start in (0, weights_ref.shape[0] - GUARD):
        weights_ref[pl.ds(start, GUARD)] = jnp.zeros((GUARD, LANES), jnp.float32)
    weights, keep = new_weights(), Rows()
    weight_rows(weights, weights_ref, plan.cone(5), depth)
    keep.stacked(keep_ref, plan.cone(5), (), HALO - 5)
    shifted, block = [new_shifted() for _ in range(3)], 0
    for n in range(3):
        held = plan.ring(6 - n, 1 - n) if n < 2 else plan.cone(4)
        block = shifted_rows(shifted[n], states_ref, held, depth, block)
    clear_pads(states_ref, block, depth)
    states = [temp, Rows(), Rows(), Rows()]
    for n, (core, given) in enumerate(
        ((first_core, first_in), (second_core, second_in), (third_core, third_in))
    ):
        tiles = (0, 1) if n < 2 else (0,)
        states[n + 1].stacked(core, plan.cone(-n - 1), (), HALO + n + 1, tiles)
        for i, r in enumerate(plan.ring(2 - n, -n - 1)):
            for t in tiles:
                states[n + 1].where[r, t] = (given, (i, t), 0)

    expand(table, weights, keep, ids, coeff, plan.cone(5), grid, rows, depth)
    for r in plan.ring(6, 1):
        put_shifted(shifted[0], r, [temp.of(r, t, depth) for t in (0, 1)])
    for r in plan.ring(2, 0):
        put_shifted(shifted[1], r, [states[1].of(r, t, depth) for t in (0, 1)])
    for r in plan.cone(1):
        put_shifted(shifted[2], r, [states[2].of(r, t, depth) for t in (0, 1)])
    states[2] = shifted[2][0]
    found = Rows()
    found.stacked(third_ref, plan.cone(3), (), HALO - 3)
    for key, place in found.where.items():
        states[3].where.setdefault(key, place)
    for n in range(STEPS):
        fresh = plan.ring(5 - n, 2 - n)
        out = states[3] if n == 2 else shifted[n + 1][0]

        def done(r, t, base, value):
            out.put(r, t, value, base)

        for part in halves(fresh, plan.middle):
            advance(weights, keep, coeff, shifted[n], part, (0, 1), depth, done)
        if n == 2:
            advance(weights, keep, coeff, shifted[n], plan.cone(0), (1,), depth, done)
            continue
        for r in fresh:
            pair = [out.of(r, t, depth) for t in (0, 1)]
            for by in (-1, 1):
                moved = lane_shift(pair, by)
                for t in (0, 1):
                    shifted[n + 1][by].put(r, t, moved[t])

    vectors, block = [], 0
    for n in range(3):
        vectors.append(Rows())
        block = vectors[n].flat(adjoint_ref, plan.cone(3 - n), depth, PAD, block)
    clear_pads(adjoint_ref, block, depth)
    drives = [None, Rows(), Rows(), vectors[0]]
    drives[1].stacked(drive_ref, plan.cone(1), (0,), HALO - 2)
    drives[2].stacked(drive_ref, plan.cone(2), (1,), HALO - 2)
    for n in range(1, 4):
        for r in plan.cone(n):
            for t in (0, 1):
                rate, inverse = rate_of(states[n].of(r, t, depth))
                factor = weights[LINKS].of(r, t, depth) * AGE_BETA
                drives[n].put(r, t, factor * rate * (inverse * inverse))
    sums = {}
    for oy in (-1, 0, 1):
        sums[oy] = Rows()
        sums[oy].stacked(sums_ref, plan.cone(2), (oy + 1,), HALO - 2)
    for n in range(3):
        vector = vectors[n]
        targets = plan.cone(2 - n)
        for t in (0, 1):
            for half in range(depth // 8):
                base = 8 * half
                totals = {}
                for source in plan.cone(3 - n):
                    reads = {oz: vector.of(source, t, 8, base - oz) for oz in (-1, 0, 1)}
                    for k, offset in enumerate(HALF_OFFSETS):
                        product = {}
                        for sign in (1, -1):
                            oz, ox, oy = (sign * o for o in offset)
                            if oz not in product:
                                weight = weights[k].of(source, t, 8, base - oz)
                                product[oz] = reads[oz] * weight
                            key = (source + ox, oy)
                            if key[0] in targets:
                                totals[key] = (
                                    totals[key] + product[oz] if key in totals else product[oz]
                                )
                    if source - 1 in targets:
                        for oy in (-1, 0, 1):
                            sums[oy].put(source - 1, t, totals.pop((source - 1, oy)), base)
        for r in targets:
            plus = lane_shift([sums[1].of(r, t, depth) for t in (0, 1)], -1)
            minus = lane_shift([sums[-1].of(r, t, depth) for t in (0, 1)], 1)
            for t in (0, 1) if n < 2 else (0,):
                result = (
                    keep.of(r, t, depth) * vector.of(r, t, depth)
                    + sums[0].of(r, t, depth)
                    + (plus[t] + minus[t])
                )
                if n < 2:
                    vectors[n + 1].put(r, t, result + drives[2 - n].of(r, t, depth))
                else:
                    adjoint_out[:, r - HALO, :] = result
    for r in plan.cone(0):
        total = None
        for n in range(3):
            term = vectors[2 - n].of(r, 0, depth) * (states[n].of(r, 0, depth) - COOL_TEMP)
            total = term if total is None else total + term
        sens_out[:, r - HALO, :] = -total * plate[:, r - HALO, :].astype(jnp.float32)


def scale_kernel(cells, parts, adjoint, sens, adjoint_out, sens_out):
    row = jnp.sum(parts[...], axis=0, keepdims=True)
    scale = cells / jnp.sum(row, axis=1, keepdims=True)
    adjoint_out[...] = adjoint[...] * scale.reshape(1, 1, 1)
    sens_out[...] = sens[...] * scale.reshape(1, 1, 1)


def pairing(count, first, ring):
    out = {}
    for i in range(first, count - 1, 2):
        out[i], out[i + 1] = i + 1, i
    if ring and 0 not in out:
        out[0], out[count - 1] = count - 1, 0
    return out


def swap(value, sizes, axis, first, ring=False):
    count_x, count_y = sizes
    partner = pairing(sizes[axis], first, ring)
    pairs = []
    for i in range(count_x):
        for j in range(count_y):
            other = partner.get((i, j)[axis])
            if other is not None:
                target = (other, j) if axis == 0 else (i, other)
                pairs.append((i * count_y + j, target[0] * count_y + target[1]))
    return lax.ppermute(value, ("gx", "gy"), pairs)


def local(initial_temp, material, plate, cooling, principal, angles, aging_scale):
    depth, rows, width = initial_temp.shape
    sizes = (lax.axis_size("gx"), lax.axis_size("gy"))
    devices = sizes[0] * sizes[1]
    f32 = jnp.float32

    def shape(*dims):
        return jax.ShapeDtypeStruct(dims, f32)

    def call(kernel, mib, out_shape, scratch=(), **specs):
        return pl.pallas_call(
            kernel,
            out_shape=out_shape,
            scratch_shapes=[
                pltpu.VMEM(dims, f32) if isinstance(dims, tuple) else dims for dims in scratch
            ],
            compiler_params=pltpu.CompilerParams(vmem_limit_bytes=mib * 2**20),
            **specs,
        )

    block = (depth, rows, LANES)
    inputs = (
        principal.T, angles.T, aging_scale[None], initial_temp, material, plate, cooling
    )
    own, pack, send_b, table = call(
        pack_kernel,
        2,
        (
            shape(3, rows, depth, LANES),
            shape(3, depth, LANES),
            shape(PAYLOAD - 3, depth, LANES),
            shape(PARTS, 8, LANES),
        ),
        (
            *(pltpu.VMEM(x.shape, x.dtype) for x in inputs),
            (8, LANES),
            pltpu.SemaphoreType.DMA((len(inputs),)),
        ),
        in_specs=[pl.BlockSpec(memory_space=pltpu.HBM)] * len(inputs),
    )(*(pltpu.with_memory_space_constraint(x, pltpu.HBM) for x in inputs))
    side_b = swap(pack, sizes, 1, 1, True)
    side_a = swap(pack, sizes, 1, 0)
    far_b = swap(send_b, sizes, 0, 1)
    mid, send_a = call(
        functools.partial(middle_kernel, sizes[1] - 1),
        2,
        (shape(3, depth, LANES), shape(PAYLOAD, depth, LANES)),
    )(own, side_a, side_b)
    got_b = swap(mid, sizes, 0, 1)
    got_a = swap(send_a, sizes, 0, 0)

    pairs = 2 * rows
    grid = (rows * sizes[0], width * sizes[1])
    halo, weights, keep, start, first_core, first_moved, second_core, second_moved, third_core, loss = call(
        functools.partial(core_kernel, grid),
        8,
        (
            shape(3, rows, depth, LANES),
            shape(*guarded_size((LINKS + 1) * pairs, depth)),
            shape(rows, 2, depth, LANES),
            shape(*padded_size(3 * pairs, depth)),
            shape(rows - 2, 2, depth, LANES),
            shape(*padded_size(3 * (pairs - 4), depth)),
            shape(rows - 4, 2, depth, LANES),
            shape(*padded_size(3 * (pairs - 8), depth)),
            shape(rows - 6, 1, depth, LANES),
            shape(8, LANES),
        ),
    )(own, mid, table)
    ext, first, second, third, part = call(
        functools.partial(front_kernel, grid),
        16,
        (
            shape(3, 2 * HALO, 2, depth, LANES),
            shape(6, 2, depth, LANES),
            shape(6, 2, depth, LANES),
            shape(6, 1, depth, LANES),
            shape(devices, LANES),
        ),
        (
            guarded_size((LINKS + 1) * 8, depth),
            (4, 2, depth, LANES),
            padded_size(3 * 12, depth),
            padded_size(3 * 12, depth),
            padded_size(3 * 12, depth),
        ),
    )(own, halo, got_b, far_b, got_a, table, weights, keep, start, first_moved, second_moved, loss)
    parts = lax.all_to_all(part, ("gx", "gy"), 0, 0, tiled=True)
    adjoint, sens = call(
        functools.partial(back_kernel, grid),
        24,
        (shape(*block), shape(*block)),
        (
            guarded_size((LINKS + 1) * (pairs + 20), depth),
            (rows + 10, 2, depth, LANES),
            padded_size(3 * (2 * 10 + 2 * 10 + pairs + 16), depth),
            (rows + 6, 2, depth, LANES),
            padded_size(3 * pairs + 4 * (3 + 2 + 1), depth),
            (3, rows + 4, 2, depth, LANES),
            (2, rows + 4, 2, depth, LANES),
        ),
    )(own, halo, ext, first_core, second_core, third_core, first, second, third, table, plate)
    return call(
        functools.partial(scale_kernel, float(depth * rows * width * devices)),
        2,
        (shape(*block), shape(*block)),
    )(parts, adjoint, sens)


def solution(mesh):
    block = P(None, "gx", "gy")
    return jax.shard_map(
        local,
        mesh=mesh,
        in_specs=(block, block, block, block, P(), P(), P()),
        out_specs=(block, block),
        check_vma=False,
    )
```
